256 devices in a mesh: seq: 64 (over z, y, core), round: 4 (over x).
Axes of the slice: x: 4, y: 4, z: 8, core: 2. Of those that a mesh axis runs over, the one named last changes fastest.
Arguments:
- queries: bfloat16 [16384, 1024], P('seq'), may hold values from -33 to 33
- keys: bfloat16 [16384, 1024], P('seq'), may hold values from -5 to 5
- values: bfloat16 [16384, 1024], P('seq'), may hold values from -6 to 6
- cotangent: bfloat16 [16384, 1024], P('seq'), may hold values from -6 to 6
- order: int32 [4, 16384], P('round', 'seq'), may hold values from 0 to 16383, as said below
- inverse: int32 [4, 16384], P('round', 'seq'), may hold values from 0 to 16383, as said below
- bucket: int32 [4, 16384], P('round'), may hold values from 0 to 63, as said below
Outputs:
- attended: bfloat16 [16384, 1024], P('seq')
- grad_queries: bfloat16 [16384, 1024], P('seq', 'round')
- grad_keys: bfloat16 [16384, 1024], P('seq', 'round')
- grad_values: bfloat16 [16384, 1024], P('seq', 'round')
The draws below stay inside these ranges and needn't reach their ends.
Inputs may be any that keep to these rules, and one draw needn't show every extreme that they name: For each round, order lists every token once. In each round the tokens of one index of seq (256 consecutive rows) take at most 6 of the sorted positions of any one index of seq, and every index of seq sends exactly 6 of its tokens to some index of seq. inverse[r, order[r, j]] = j. Along a round's sorted positions the bucket numbers never fall, except that a last run of 1 to 128 positions at the end of the sequence carries bucket 0, the bucket of the first position.
All inputs are finite; a program needn't handle non-finite values.
Results may differ from the reference program's by a relative error of at most 0.014.
Values may be sent and summed in bfloat16 or wider, within the bound.
A program may use at most 64 MiB of HBM per device.

```python
import math
import jax
import jax.numpy as jnp
from jax import lax

HEADS = 8
HEAD_DIM = 128
FEATS = 1024
SPAN = 128
ROUNDS = 4
TOK_DEV = 256
SEQLEN = 16384
N_SEQ = 64


def routing_round(round_key):
    blocks = N_SEQ
    base = TOK_DEV // N_SEQ
    spread = base // 2
    step_key, label_key, shuffle_key, tie_key = jax.random.split(round_key, 4)
    steps = jax.random.randint(step_key, (blocks,), 0, spread + 1)
    steps = steps.at[0].set(spread).at[blocks - 1].set(0)
    offsets = steps - jnp.roll(steps, 1)
    relabel = jax.random.permutation(label_key, blocks)
    senders = jnp.arange(blocks)
    counts = base + offsets[(relabel[None, :] - senders[:, None]) % blocks]
    bounds = jnp.cumsum(counts, axis=1)
    local = jax.vmap(lambda piece: jax.random.permutation(piece, TOK_DEV))(jax.random.split(shuffle_key, blocks))
    places = jnp.arange(TOK_DEV)
    target = jnp.sum((places[None, :, None] >= bounds[:, None, :]).astype(jnp.int32), axis=2)
    tokens = senders[:, None] * TOK_DEV + local
    length = blocks * TOK_DEV
    target_of = jnp.zeros((length,), jnp.int32).at[tokens.reshape(-1)].set(target.reshape(-1).astype(jnp.int32))
    ties = jax.random.permutation(tie_key, length).astype(jnp.int32)
    ordering = jnp.argsort(target_of * length + ties, stable=True).astype(jnp.int32)
    inverted = jnp.zeros((length,), jnp.int32).at[ordering].set(jnp.arange(length, dtype=jnp.int32))
    return (ordering, inverted)


def routing_tables(key):
    pairs = [routing_round(jax.random.fold_in(key, 100 + rnd)) for rnd in range(ROUNDS)]
    return (jnp.stack([entry[0] for entry in pairs]), jnp.stack([entry[1] for entry in pairs]))


def draw_order(key, part):
    return routing_tables(jax.random.fold_in(key, 5))[0]


def draw_inverse(key, part):
    return routing_tables(jax.random.fold_in(key, 5))[1]


def draw_bucket(key, part):
    flag_key = jax.random.fold_in(key, 31)
    tail_key = jax.random.fold_in(key, 32)
    starts = (jax.random.randint(flag_key, (ROUNDS, SEQLEN), 0, 256) == 0).astype(jnp.int32)
    starts = starts.at[:, 0].set(0)
    labels = jnp.cumsum(starts, axis=1).astype(jnp.int32)
    labels = jnp.minimum(labels, SEQLEN // 256 - 1)
    tail = jax.random.randint(tail_key, (ROUNDS, 1), 1, SPAN + 1)
    position = jnp.arange(SEQLEN, dtype=jnp.int32)[None, :]
    labels = jnp.where(position >= SEQLEN - tail - 1, SEQLEN // 256 - 1, labels)
    return jnp.where(position >= SEQLEN - tail, 0, labels).astype(jnp.int32)


def key_rows(key):
    return jnp.clip(jax.random.normal(jax.random.fold_in(key, 21), (SEQLEN, FEATS), jnp.float32), -5.0, 5.0)


def draw_keys(key, part):
    return key_rows(key).astype(jnp.bfloat16)


def draw_queries(key, part):
    drawn = jnp.clip(jax.random.normal(jax.random.fold_in(key, 22), (SEQLEN, FEATS), jnp.float32), -5.0, 5.0)
    return drawn.astype(jnp.bfloat16)


def steps_of(stream_key, shape, cuts, least, high):
    factor_of, own = 1.0, jax.random.fold_in(stream_key, 6)
    for dim, shards_of in cuts:
        steps = jnp.exp(jax.random.uniform(jax.random.fold_in(own, dim), (shards_of,), jnp.float32, least / len(cuts), high / len(cuts)))
        factor_of = factor_of * jnp.repeat(steps, shape[dim] // shards_of).reshape([-1 if axis == dim else 1 for axis in range(len(shape))])
    return factor_of


def scatter_about(own_key, shape, scale, bound, cuts=(), held_as=jnp.bfloat16):
    values = scale * jax.random.normal(own_key, shape, jnp.float32)
    if cuts:
        values = values * steps_of(own_key, shape, cuts, -0.22, 0.18)
    return jnp.clip(values, -bound, bound).astype(held_as)


def setup_inputs(seed: int = 0) -> dict:
    seeds = jax.random.split(jax.random.key(seed), 8)
    return {
        "queries": draw_queries(jax.random.fold_in(seeds[7], 71), 0),
        "keys": draw_keys(jax.random.fold_in(seeds[7], 71), 0),
        "values": scatter_about(seeds[2], (SEQLEN, FEATS), 1.0, 6.0, ((0, 64),)),
        "cotangent": scatter_about(seeds[3], (SEQLEN, FEATS), 1.0, 6.0, ((0, 64),)),
        "order": draw_order(jax.random.fold_in(seeds[7], 71), 0),
        "inverse": draw_inverse(jax.random.fold_in(seeds[7], 71), 0),
        "bucket": draw_bucket(jax.random.fold_in(seeds[7], 71), 0),
    }


NEG = -1e30


def grouped(function, arrays):
    total = arrays[0].shape[0]
    group = math.gcd(total, 8)
    shaped = tuple(entry.reshape((total // group, group) + entry.shape[1:]) for entry in arrays)
    results = lax.map(function, shaped)
    return tuple(entry.reshape((total,) + entry.shape[2:]) for entry in results)


def heads_of(rows):
    return rows.reshape(rows.shape[0], rows.shape[1], HEADS, HEAD_DIM).astype(jnp.float32)


def block_scores(query_block, key_window, query_bucket, key_bucket):
    scores = jnp.einsum("cqhd,ckhd->chqk", heads_of(query_block), heads_of(key_window)) * (HEAD_DIM ** -0.5)
    allowed = (query_bucket[:, :, None] == key_bucket[:, None, :])[:, None]
    return scores, allowed


def forward_blocks(arrays):
    query_block, key_window, value_window, query_bucket, key_bucket = arrays
    blocks, width = query_block.shape[0], query_block.shape[1]
    scores, allowed = block_scores(query_block, key_window, query_bucket, key_bucket)
    peak = jnp.max(jnp.where(allowed, scores, NEG), axis=-1, keepdims=True)
    expon = jnp.exp(jnp.where(allowed, scores - peak, NEG))
    total = jnp.sum(expon, axis=-1, keepdims=True)
    weights = (expon / total).astype(jnp.bfloat16)
    output = jnp.einsum("chqk,ckhd->cqhd", weights.astype(jnp.float32), heads_of(value_window))
    logsum = jnp.transpose((peak + jnp.log(total))[..., 0], (0, 2, 1))
    return output.reshape(blocks, width, HEADS * HEAD_DIM), logsum


def backward_blocks(arrays):
    query_block, key_window, value_window, grad_block, query_bucket, key_bucket, logsum, delta = arrays
    blocks, width = query_block.shape[0], query_block.shape[1]
    scale = HEAD_DIM ** -0.5
    scores, allowed = block_scores(query_block, key_window, query_bucket, key_bucket)
    lse_block = jnp.transpose(logsum, (0, 2, 1))[..., None]
    delta_block = jnp.transpose(delta, (0, 2, 1))[..., None]
    prob = jnp.exp(jnp.where(allowed, scores - lse_block, NEG))
    prob_low = lax.optimization_barrier(prob.astype(jnp.bfloat16)).astype(jnp.float32)
    grad_heads = heads_of(grad_block)
    value_grad = jnp.einsum("chqk,cqhd->ckhd", prob_low, grad_heads)
    prob_grad = jnp.einsum("cqhd,ckhd->chqk", grad_heads, heads_of(value_window))
    score_low = (prob * (prob_grad - delta_block)).astype(jnp.bfloat16)
    score_grad = lax.optimization_barrier(score_low).astype(jnp.float32)
    query_grad = jnp.einsum("chqk,ckhd->cqhd", score_grad, heads_of(key_window)) * scale
    key_grad = jnp.einsum("chqk,cqhd->ckhd", score_grad, heads_of(query_block)) * scale
    feats = HEADS * HEAD_DIM
    return (query_grad.reshape(blocks, width, feats), key_grad.reshape(blocks, 2 * width, feats),
            value_grad.reshape(blocks, 2 * width, feats))


def join_rounds(logsum_a, output_a, logsum_b, output_b):
    top = jnp.maximum(logsum_a, logsum_b)
    weight_a = jnp.exp(logsum_a - top)
    weight_b = jnp.exp(logsum_b - top)
    total = weight_a + weight_b
    rows = output_a.shape[0]
    mixed = (output_a.reshape(rows, HEADS, HEAD_DIM) * weight_a[..., None]
             + output_b.reshape(rows, HEADS, HEAD_DIM) * weight_b[..., None]) / total[..., None]
    return top + jnp.log(total), mixed.reshape(rows, HEADS * HEAD_DIM)


def reference(queries, keys, values, cotangent, order, inverse, bucket):
    blocks = SEQLEN // SPAN
    feats = HEADS * HEAD_DIM

    def spanned(rows):
        return rows.reshape((blocks, SPAN) + rows.shape[1:])

    def window(rows):
        return jnp.concatenate([jnp.roll(rows, 1, axis=0), rows], axis=1)

    running_lse = None
    running_out = None
    for rnd in range(ROUNDS):
        index = order[rnd].astype(jnp.int32)
        back = inverse[rnd].astype(jnp.int32)
        query_block = spanned(jnp.take(queries, index, axis=0))
        key_block = spanned(jnp.take(keys, index, axis=0))
        value_block = spanned(jnp.take(values, index, axis=0))
        query_bucket = bucket[rnd].reshape(blocks, SPAN)
        output, logsum = grouped(forward_blocks, (query_block, window(key_block), window(value_block),
                                                  query_bucket, window(query_bucket)))
        out_tok = jnp.take(output.reshape(SEQLEN, feats), back, axis=0)
        lse_tok = jnp.take(logsum.reshape(SEQLEN, HEADS), back, axis=0)
        if running_lse is None:
            running_lse, running_out = lse_tok, out_tok
        else:
            running_lse, running_out = join_rounds(running_lse, running_out, lse_tok, out_tok)
    combined = running_out
    attended = combined.astype(jnp.bfloat16)
    delta = jnp.sum(cotangent.astype(jnp.float32).reshape(SEQLEN, HEADS, HEAD_DIM)
                    * combined.reshape(SEQLEN, HEADS, HEAD_DIM), axis=-1)
    summed = jnp.zeros((SEQLEN, 3 * feats), jnp.float32)
    for rnd in range(ROUNDS):
        index = order[rnd].astype(jnp.int32)
        back = inverse[rnd].astype(jnp.int32)
        query_block = spanned(jnp.take(queries, index, axis=0))
        key_block = spanned(jnp.take(keys, index, axis=0))
        value_block = spanned(jnp.take(values, index, axis=0))
        grad_block = spanned(jnp.take(cotangent, index, axis=0))
        lse_block = spanned(jnp.take(running_lse, index, axis=0))
        delta_block = spanned(jnp.take(delta, index, axis=0))
        query_bucket = bucket[rnd].reshape(blocks, SPAN)
        query_grad, key_grad, value_grad = grouped(backward_blocks, (
            query_block, window(key_block), window(value_block), grad_block,
            query_bucket, window(query_bucket), lse_block, delta_block))
        key_total = key_grad[:, SPAN:] + jnp.roll(key_grad[:, :SPAN], -1, axis=0)
        value_total = value_grad[:, SPAN:] + jnp.roll(value_grad[:, :SPAN], -1, axis=0)
        round_grads = jnp.concatenate([query_grad, key_total, value_total], axis=-1)
        round_grads = round_grads.reshape(SEQLEN, 3 * feats).astype(jnp.bfloat16)
        summed = summed + jnp.take(round_grads, back, axis=0).astype(jnp.float32)
    final = summed.astype(jnp.bfloat16)
    return attended, final[:, :feats], final[:, feats:2 * feats], final[:, 2 * feats:]
```

```python
import functools

import jax
import jax.numpy as jnp
from jax import lax
from jax.experimental import pallas as pl
from jax.experimental.pallas import tpu as pltpu
from jax.sharding import PartitionSpec as P

HEADS = 8
HEAD_DIM = 128
SPAN = 128
TOK = 256
SLOT = 6
GRP = 8
CHUNK = GRP * SLOT
MSG = GRP * CHUNK
ROUNDS = 4
ROWS = GRP * TOK
NBLK = ROWS // SPAN
NEG = -1e30
SCALE = HEAD_DIM ** (-0.5)
f32 = jnp.float32
bf16 = jnp.bfloat16
i32 = jnp.int32
ANY = pl.ANY


def here():
    x = lax.axis_index("round")
    s = lax.axis_index("seq")
    return x, lax.div(s, GRP), lax.rem(s, GRP)


def device(x, z, k):
    return {"seq": z * GRP + k, "round": x}


def remote(src, dst, send, recv, target):
    return pltpu.make_async_remote_copy(
        src_ref=src, dst_ref=dst, send_sem=send, recv_sem=recv,
        device_id=target, device_id_type=pl.DeviceIdType.MESH,
    )


def signal(sem, target):
    pl.semaphore_signal(sem, inc=1, device_id=target, device_id_type=pl.DeviceIdType.MESH)


def greet_line(barrier, x, z, k):
    me = x * GRP + z

    def go(i, c):
        o = lax.rem(me + i, 4 * GRP)
        signal(barrier, device(lax.div(o, GRP), lax.rem(o, GRP), k))
        return c

    lax.fori_loop(1, 4 * GRP, go, 0)


def greet_plane(barrier, x, z, k):
    me = x * GRP + k

    def go(i, c):
        o = lax.rem(me + i, 4 * GRP)
        signal(barrier, device(lax.div(o, GRP), z, lax.rem(o, GRP)))
        return c

    lax.fori_loop(1, 4 * GRP, go, 0)


def loop(lo, hi, body):
    def go(i, c):
        body(i)
        return c

    lax.fori_loop(lo, hi, go, 0)


def spread_kernel(q, k_, v, g, sidx, ridx, zin, sall, rall,
                  buf, zs, zr, ss, sr, rs, rr, ls):
    x, z, k = here()
    barrier = pltpu.get_barrier_semaphore()
    greet_line(barrier, x, z, k)
    mine = (z == k).astype(i32)

    def greet_pos(i):
        @pl.when(jnp.logical_or(z != k, i != z))
        def _():
            signal(barrier, device(x, i, z))

        @pl.when(jnp.logical_or(z != k, i != k))
        def _():
            signal(barrier, device(x, k, i))

    loop(0, GRP, greet_pos)
    pl.semaphore_wait(barrier, 4 * GRP - 1 + 2 * (GRP - mine))

    def cols(ref, h):
        return ref.at[:, pl.ds(pl.multiple_of(h * HEAD_DIM, HEAD_DIM), HEAD_DIM)]

    for t, ref in enumerate((q, k_, v, g)):
        @pl.when(x == t)
        def _(ref=ref):
            def go(i):
                o = lax.rem(z + i, GRP)
                remote(cols(ref, o), zin.at[z], zs.at[o], zr.at[z], device(x, o, k)).start()

            loop(1, GRP, go)
            pltpu.make_async_copy(cols(ref, z), buf, ls.at[0]).start()

    me = x * GRP + z

    def send_idx(i):
        o = lax.rem(me + i, 4 * GRP)
        remote(sidx, sall.at[me], ss.at[o], sr.at[me],
               device(lax.div(o, GRP), lax.rem(o, GRP), k)).start()

    loop(1, 4 * GRP, send_idx)
    pltpu.make_async_copy(sidx, sall.at[me], ls.at[1]).start()

    def send_pos(i):
        @pl.when(jnp.logical_or(z != k, i != z))
        def _():
            remote(ridx, rall.at[k], rs.at[i], rr.at[k], device(x, i, z)).start()

    loop(0, GRP, send_pos)

    @pl.when(z == k)
    def _():
        pltpu.make_async_copy(ridx, rall.at[k], ls.at[2]).start()
        pltpu.make_async_copy(ridx, rall.at[k], ls.at[2]).wait()

    pltpu.make_async_copy(cols(q, z), buf, ls.at[0]).wait()
    pltpu.make_async_copy(buf, zin.at[z], ls.at[3]).start()
    pltpu.make_async_copy(sidx, sall.at[me], ls.at[1]).wait()

    def wait_idx(i):
        o = lax.rem(me + i, 4 * GRP)
        cp = remote(sidx, sall.at[o], ss.at[o], sr.at[o],
                    device(lax.div(o, GRP), lax.rem(o, GRP), k))
        cp.wait_send()
        cp.wait_recv()

    loop(1, 4 * GRP, wait_idx)

    def wait_pos(i):
        @pl.when(jnp.logical_or(z != k, i != z))
        def _():
            remote(ridx, rall.at[k], rs.at[i], rr.at[i], device(x, i, z)).wait_send()

        @pl.when(jnp.logical_or(z != k, i != k))
        def _():
            remote(ridx, rall.at[i], rs.at[i], rr.at[i], device(x, k, i)).wait_recv()

    loop(0, GRP, wait_pos)

    def wait_rows(i):
        o = lax.rem(z + i, GRP)
        cp = remote(cols(q, o), zin.at[o], zs.at[o], zr.at[o], device(x, o, k))
        cp.wait_send()
        cp.wait_recv()

    loop(1, GRP, wait_rows)
    pltpu.make_async_copy(buf, zin.at[z], ls.at[3]).wait()


def spread(q, k, v, g, sidx, ridx):
    n = 4 * GRP
    return pl.pallas_call(
        spread_kernel,
        out_shape=(
            jax.ShapeDtypeStruct((GRP, TOK, HEAD_DIM), bf16),
            jax.ShapeDtypeStruct((n, 1, TOK), i32),
            jax.ShapeDtypeStruct((GRP, 1, TOK), i32),
        ),
        in_specs=[pl.BlockSpec(memory_space=ANY)] * 4 + [pl.BlockSpec(memory_space=pltpu.VMEM)] * 2,
        out_specs=(
            pl.BlockSpec(memory_space=ANY),
            pl.BlockSpec(memory_space=pltpu.VMEM),
            pl.BlockSpec(memory_space=pltpu.VMEM),
        ),
        scratch_shapes=[
            pltpu.VMEM((TOK, HEAD_DIM), bf16),
            pltpu.SemaphoreType.DMA((GRP,)),
            pltpu.SemaphoreType.DMA((GRP,)),
            pltpu.SemaphoreType.DMA((n,)),
            pltpu.SemaphoreType.DMA((n,)),
            pltpu.SemaphoreType.DMA((GRP,)),
            pltpu.SemaphoreType.DMA((GRP,)),
            pltpu.SemaphoreType.DMA((4,)),
        ],
        compiler_params=pltpu.CompilerParams(collective_id=0, has_side_effects=True),
        name="spread",
    )(q, k, v, g, sidx, ridx)


def plane_kernel(src, dst, buf, ss, rs, ls):
    x, z, k = here()
    me = x * GRP + k
    barrier = pltpu.get_barrier_semaphore()
    greet_plane(barrier, x, z, k)
    pl.semaphore_wait(barrier, 4 * GRP - 1)

    def other(i):
        o = lax.rem(me + i * 11, 4 * GRP)
        return o, device(lax.div(o, GRP), z, lax.rem(o, GRP))

    def go(i):
        o, target = other(i)
        remote(src.at[o], dst.at[me], ss.at[o], rs.at[me], target).start()

    loop(1, 4 * GRP, go)
    pltpu.make_async_copy(src.at[me], buf, ls.at[0]).start()
    pltpu.make_async_copy(src.at[me], buf, ls.at[0]).wait()
    pltpu.make_async_copy(buf, dst.at[me], ls.at[1]).start()

    def end(i):
        o, target = other(i)
        cp = remote(src.at[o], dst.at[o], ss.at[o], rs.at[o], target)
        cp.wait_send()
        cp.wait_recv()

    loop(1, 4 * GRP, end)
    pltpu.make_async_copy(buf, dst.at[me], ls.at[1]).wait()


def plane_exchange(packed, ident, name):
    return pl.pallas_call(
        plane_kernel,
        out_shape=jax.ShapeDtypeStruct(packed.shape, packed.dtype),
        in_specs=[pl.BlockSpec(memory_space=ANY)],
        out_specs=pl.BlockSpec(memory_space=ANY),
        scratch_shapes=[
            pltpu.VMEM(packed.shape[1:], packed.dtype),
            pltpu.SemaphoreType.DMA((4 * GRP,)),
            pltpu.SemaphoreType.DMA((4 * GRP,)),
            pltpu.SemaphoreType.DMA((2,)),
        ],
        compiler_params=pltpu.CompilerParams(collective_id=ident, has_side_effects=True),
        name=name,
    )(packed)


def row_onehot(idx, count):
    places = lax.broadcasted_iota(i32, (count, TOK), 0)
    return jnp.where(places == idx, 1.0, 0.0).astype(bf16)


def col_of(idx):
    wide = jnp.broadcast_to(idx.astype(f32), (128, TOK))
    return jnp.concatenate([wide[:, :128].T, wide[:, 128:].T], axis=0).astype(i32)


def col_onehot(idx, count):
    col = col_of(idx)
    lanes = lax.broadcasted_iota(i32, (TOK, 128), 1)
    parts = [jnp.where(col == lanes + m, 1.0, 0.0).astype(bf16) for m in range(0, count, 128)]
    return jnp.concatenate(parts, axis=1)


def dot(a, b):
    return jnp.dot(a, b, preferred_element_type=f32)


def dot_nt(a, b):
    return lax.dot_general(a, b, (((1,), (1,)), ((), ())), preferred_element_type=f32)


def dot_tn(a, b):
    return lax.dot_general(a, b, (((0,), (0,)), ((), ())), preferred_element_type=f32)


def pack_kernel(zin, sall, out):
    i = pl.program_id(0)
    for r in range(ROUNDS):
        onehot = row_onehot(sall[r * GRP + i], MSG)
        rows = dot(onehot, zin[0]).astype(bf16)
        out[r * GRP:(r + 1) * GRP, 0] = rows.reshape(GRP, CHUNK, HEAD_DIM)


def pack_tokens(zin, sall):
    return pl.pallas_call(
        pack_kernel,
        grid=(GRP,),
        out_shape=jax.ShapeDtypeStruct((4 * GRP, GRP, CHUNK, HEAD_DIM), bf16),
        in_specs=[
            pl.BlockSpec((1, TOK, HEAD_DIM), lambda i: (i, 0, 0)),
            pl.BlockSpec((4 * GRP, 1, TOK), lambda i: (0, 0, 0)),
        ],
        out_specs=pl.BlockSpec((4 * GRP, 1, CHUNK, HEAD_DIM), lambda i: (0, i, 0, 0)),
        name="pack_tokens",
    )(zin, sall)


def unpack_kernel(recv, swap, rall, rows, mid):
    def first(g):
        parts = [recv[t * GRP + g].reshape(MSG, HEAD_DIM) for t in range(4)]
        moved = dot(swap[...], jnp.concatenate(parts, axis=1)).astype(bf16)
        mid[:, g] = moved.reshape(GRP, CHUNK, 4 * HEAD_DIM)

    loop(0, GRP, first)

    def second(d):
        onehot = col_onehot(rall[d], MSG)
        rows[d] = dot(onehot, mid[d].reshape(MSG, 4 * HEAD_DIM)).astype(bf16)

    loop(0, GRP, second)


def unpack_rows(recv, swap, rall):
    return pl.pallas_call(
        unpack_kernel,
        out_shape=jax.ShapeDtypeStruct((GRP, TOK, 4 * HEAD_DIM), bf16),
        scratch_shapes=[pltpu.VMEM((GRP, GRP, CHUNK, 4 * HEAD_DIM), bf16)],
        name="unpack_rows",
    )(recv, swap, rall)


def allowed_of(bk, b):
    own = bk[b + 1]
    prev = bk[b]
    col = jnp.broadcast_to(own, (SPAN, SPAN)).T
    return jnp.concatenate([col == prev, col == own], axis=1)


def three(a):
    hi = a.astype(bf16)
    left = a - hi.astype(f32)
    mid = left.astype(bf16)
    low = (left - mid.astype(f32)).astype(bf16)
    return hi.astype(f32), mid.astype(f32), low.astype(f32)


def window(rows, tail, b):
    own = rows[b]
    before = jnp.where(b == 0, tail[...], rows[jnp.maximum(b - 1, 0)][:, HEAD_DIM:3 * HEAD_DIM])
    keys = jnp.concatenate([before[:, :HEAD_DIM], own[:, HEAD_DIM:2 * HEAD_DIM]], axis=0)
    vals = jnp.concatenate([before[:, HEAD_DIM:], own[:, 2 * HEAD_DIM:3 * HEAD_DIM]], axis=0)
    return own[:, :HEAD_DIM], keys, vals, own[:, 3 * HEAD_DIM:]


def forward_kernel(rows, tail, bk, swap, rall, out, stat, mid):
    lane = lax.rem(lax.broadcasted_iota(i32, (SPAN, 128), 1), 8)

    def block(b):
        query, keys, vals, grad = window(rows, tail, b)
        allowed = allowed_of(bk, b)
        scores = dot_nt(query, keys) * SCALE
        scores = jnp.where(allowed, scores, NEG)
        peak = jnp.max(scores, axis=-1, keepdims=True)
        expon = jnp.where(allowed, jnp.exp(scores - peak), 0.0)
        total = jnp.sum(expon, axis=-1, keepdims=True)
        weights = (expon / total).astype(bf16)
        output = dot(weights, vals)
        lse = peak + jnp.log(total)
        inner = jnp.sum(output * grad.astype(f32), axis=-1, keepdims=True)
        value = jnp.zeros((SPAN, 128), f32)
        for n, piece in enumerate(three(lse) + three(inner)):
            value = jnp.where(lane == n, piece, value)
        stat[b] = value.astype(bf16)

    loop(0, NBLK, block)
    group = lax.div(lax.broadcasted_iota(i32, (CHUNK, 128), 1), 8)

    def pack(d):
        onehot = row_onehot(rall[d], MSG)
        both = jnp.concatenate([stat[2 * d], stat[2 * d + 1]], axis=0)
        moved = dot(onehot, both)
        value = jnp.zeros((CHUNK, 128), f32)
        for g in range(GRP):
            value = jnp.where(group == g, moved[g * CHUNK:(g + 1) * CHUNK], value)
        mid[d] = value.astype(bf16)

    loop(0, GRP, pack)
    final = dot(swap[...], mid[...].reshape(MSG, 128))
    out[...] = final.T[:8 * GRP].reshape(GRP, 8, MSG)


def forward(rows, tail, bk, swap, rall):
    return pl.pallas_call(
        forward_kernel,
        out_shape=jax.ShapeDtypeStruct((GRP, 8, MSG), f32),
        scratch_shapes=[pltpu.VMEM((NBLK, SPAN, 128), bf16), pltpu.VMEM((GRP, CHUNK, 128), bf16)],
        name="forward",
    )(rows, tail, bk, swap, rall)


def stats_kernel(sent, sall, back, got, table, across, reply, s1, r1, s2, r2, s3, r3):
    x, z, k = here()
    barrier = pltpu.get_barrier_semaphore()

    def greet_k(i):
        signal(barrier, device(x, z, lax.rem(k + i, GRP)))

    def greet_x(i):
        signal(barrier, device(lax.rem(x + i, ROUNDS), z, k))

    loop(1, GRP, greet_k)
    loop(1, ROUNDS, greet_x)
    pl.semaphore_wait(barrier, GRP + ROUNDS - 2)

    def go1(i):
        o = lax.rem(k + i, GRP)
        remote(sent.at[o], got.at[k], s1.at[o], r1.at[k], device(x, z, o)).start()

    loop(1, GRP, go1)
    got[k] = sent[k]

    def fill(i):
        onehot = row_onehot(sall[x * GRP + i], MSG)
        table[:, i] = onehot.reshape(GRP, CHUNK, TOK)

    loop(0, GRP, fill)

    def end1(i):
        o = lax.rem(k + i, GRP)
        cp = remote(sent.at[o], got.at[o], s1.at[o], r1.at[o], device(x, z, o))
        cp.wait_send()
        cp.wait_recv()

    loop(1, GRP, end1)
    chunk_of = lax.broadcasted_iota(i32, (8, MSG), 1)
    row_of = lax.broadcasted_iota(i32, (8, MSG), 0)
    start = row_of * CHUNK
    keep = jnp.logical_and(chunk_of >= start, chunk_of < start + CHUNK)

    def collect(o, total):
        part = got[o]
        wide = [jnp.where(keep, jnp.broadcast_to(part[n:n + 1], (8, MSG)), 0.0) for n in range(6)]
        return total + dot(jnp.concatenate(wide, axis=0).astype(bf16), table[o].reshape(MSG, TOK))

    tok = lax.fori_loop(0, GRP, collect, jnp.zeros((48, TOK), f32))
    across[x, 0] = tok[0:8] + tok[8:16] + tok[16:24]
    across[x, 1] = tok[24:32] + tok[32:40] + tok[40:48]

    def go2(i):
        o = lax.rem(x + i, ROUNDS)
        remote(across.at[x], across.at[x], s2.at[o], r2.at[x], device(o, z, k)).start()

    loop(1, ROUNDS, go2)

    def end2(i):
        o = lax.rem(x + i, ROUNDS)
        cp = remote(across.at[x], across.at[o], s2.at[o], r2.at[o], device(o, z, k))
        cp.wait_send()
        cp.wait_recv()

    loop(1, ROUNDS, end2)
    lses = [across[r, 0] for r in range(ROUNDS)]
    top = jnp.maximum(jnp.maximum(lses[0], lses[1]), jnp.maximum(lses[2], lses[3]))
    exps = [jnp.exp(a - top) for a in lses]
    total = (exps[0] + exps[1]) + (exps[2] + exps[3])
    joint = top + jnp.log(total)
    delta = sum(exps[r] * across[r, 1] for r in range(ROUNDS)) / total
    pieces = jnp.concatenate(three(joint) + three(delta), axis=0).astype(bf16)

    def answer(o):
        wide = dot_nt(pieces, table[o].reshape(MSG, TOK))
        parts = [jnp.sum(jnp.where(keep, wide[n * 8:(n + 1) * 8], 0.0), axis=0, keepdims=True)
                 for n in range(6)]
        parts += [jnp.zeros((2, MSG), f32)]
        reply[o] = jnp.concatenate(parts, axis=0)

    loop(0, GRP, answer)

    def go3(i):
        o = lax.rem(k + i, GRP)
        remote(reply.at[o], back.at[k], s3.at[o], r3.at[k], device(x, z, o)).start()

    loop(1, GRP, go3)
    back[k] = reply[k]

    def end3(i):
        o = lax.rem(k + i, GRP)
        cp = remote(reply.at[o], back.at[o], s3.at[o], r3.at[o], device(x, z, o))
        cp.wait_send()
        cp.wait_recv()

    loop(1, GRP, end3)


def stats(sent, sall):
    dma = pltpu.SemaphoreType.DMA
    return pl.pallas_call(
        stats_kernel,
        out_shape=jax.ShapeDtypeStruct((GRP, 8, MSG), f32),
        in_specs=[pl.BlockSpec(memory_space=pltpu.VMEM)] * 2,
        out_specs=pl.BlockSpec(memory_space=pltpu.VMEM),
        scratch_shapes=[
            pltpu.VMEM((GRP, 8, MSG), f32),
            pltpu.VMEM((GRP, GRP, CHUNK, TOK), bf16),
            pltpu.VMEM((ROUNDS, 2, GRP, TOK), f32),
            pltpu.VMEM((GRP, 8, MSG), f32),
            dma((GRP,)), dma((GRP,)), dma((ROUNDS,)), dma((ROUNDS,)), dma((GRP,)), dma((GRP,)),
        ],
        compiler_params=pltpu.CompilerParams(collective_id=2, has_side_effects=True),
        name="stats",
    )(sent, sall)


def backward_kernel(rows, tail, bk, back, swap, rall, outq, outkv, mid):
    flat = back[...].reshape(8 * GRP, MSG)
    wide = jnp.concatenate([flat, jnp.zeros((128 - 8 * GRP, MSG), f32)], axis=0)
    mid[...] = dot(swap[...], wide.T.astype(bf16)).astype(bf16).reshape(GRP, CHUNK, 128)
    group = lax.div(lax.broadcasted_iota(i32, (CHUNK, 128), 1), 8)
    lane = lax.rem(lax.broadcasted_iota(i32, (TOK, 128), 1), 8)
    outkv[0] = jnp.zeros((SPAN, 2 * HEAD_DIM), f32)

    def body(d):
        part = mid[d].astype(f32)
        spread_rows = jnp.concatenate(
            [jnp.where(group == g, part, 0.0) for g in range(GRP)], axis=0
        ).astype(bf16)
        found = dot(col_onehot(rall[d], MSG), spread_rows)
        joint = jnp.sum(jnp.where(lane < 3, found, 0.0), axis=-1, keepdims=True)
        delta = jnp.sum(jnp.where(jnp.logical_and(lane >= 3, lane < 6), found, 0.0), axis=-1,
                        keepdims=True)
        for half in range(2):
            b = 2 * d + half
            query, keys, vals, grad = window(rows, tail, b)
            allowed = allowed_of(bk, b)
            scores = dot_nt(query, keys) * SCALE
            lse = joint[half * SPAN:(half + 1) * SPAN]
            prob = jnp.exp(jnp.where(allowed, scores - lse, NEG))
            low = prob.astype(bf16)
            value_grad = dot_tn(low, grad)
            prob_grad = dot_nt(grad, vals)
            score_grad = (prob * (prob_grad - delta[half * SPAN:(half + 1) * SPAN])).astype(bf16)
            query_grad = dot(score_grad, keys) * SCALE
            key_grad = dot_tn(score_grad, query) * SCALE
            outq[b] = jnp.concatenate([dot(low, vals), query_grad], axis=1).astype(bf16)
            both = jnp.concatenate([key_grad, value_grad], axis=1)
            outkv[b] = outkv[b] + both[:SPAN]
            outkv[b + 1] = both[SPAN:]

    loop(0, GRP, body)


def backward(rows, tail, bk, back, swap, rall):
    return pl.pallas_call(
        backward_kernel,
        out_shape=(
            jax.ShapeDtypeStruct((NBLK, SPAN, 2 * HEAD_DIM), bf16),
            jax.ShapeDtypeStruct((NBLK + 1, SPAN, 2 * HEAD_DIM), f32),
        ),
        scratch_shapes=[pltpu.VMEM((GRP, CHUNK, 128), bf16)],
        name="backward",
    )(rows, tail, bk, back, swap, rall)


def repack_kernel(zref, outq, outkv, spill, swap, rall, out, mid):
    z = zref[0]

    def first(d):
        onehot = row_onehot(rall[d], MSG)
        upper = jnp.concatenate([outq[2 * d], outkv[2 * d + 1].astype(bf16)], axis=1)
        last = outkv[2 * d + 2] + jnp.where(d == GRP - 1, spill[...].astype(f32), 0.0)
        lower = jnp.concatenate([outq[2 * d + 1], last.astype(bf16)], axis=1)
        moved = dot(onehot, jnp.concatenate([upper, lower], axis=0)).astype(bf16)
        mid[:, d] = moved.reshape(GRP, CHUNK, 4 * HEAD_DIM)

    loop(0, GRP, first)

    def second(g):
        moved = dot(swap[...], mid[g].reshape(MSG, 4 * HEAD_DIM)).astype(bf16)
        for i in range(GRP):
            for t in range(4):
                owner = lax.rem(t - i - z + 16, 4)
                out[owner * GRP + g, i] = moved[i * CHUNK:(i + 1) * CHUNK,
                                                t * HEAD_DIM:(t + 1) * HEAD_DIM]

    loop(0, GRP, second)


def repack(z, outq, outkv, spill, swap, rall):
    vm = pl.BlockSpec(memory_space=pltpu.VMEM)
    return pl.pallas_call(
        repack_kernel,
        out_shape=jax.ShapeDtypeStruct((4 * GRP, GRP, CHUNK, HEAD_DIM), bf16),
        in_specs=[pl.BlockSpec(memory_space=pltpu.SMEM), vm, vm, vm, vm, vm],
        out_specs=vm,
        scratch_shapes=[pltpu.VMEM((GRP, GRP, CHUNK, 4 * HEAD_DIM), bf16)],
        name="repack",
    )(z, outq, outkv, spill, swap, rall)


def settle_kernel(recv, sall, out):
    i = pl.program_id(0)
    total = jnp.zeros((TOK, HEAD_DIM), f32)
    for r in range(ROUNDS):
        onehot = col_onehot(sall[r * GRP + i], MSG)
        total = total + dot(onehot, recv[r * GRP:(r + 1) * GRP, 0].reshape(MSG, HEAD_DIM))
    out[0] = total.astype(bf16)


def settle(recv, sall):
    return pl.pallas_call(
        settle_kernel,
        grid=(GRP,),
        out_shape=jax.ShapeDtypeStruct((GRP, TOK, HEAD_DIM), bf16),
        in_specs=[
            pl.BlockSpec((4 * GRP, 1, CHUNK, HEAD_DIM), lambda i: (0, i, 0, 0)),
            pl.BlockSpec((4 * GRP, 1, TOK), lambda i: (0, 0, 0)),
        ],
        out_specs=pl.BlockSpec((1, TOK, HEAD_DIM), lambda i: (i, 0, 0)),
        name="settle",
    )(recv, sall)


def home_kernel(rows, att, gq, gk, gv, buf, ss, ra, rg, ls):
    x, z, k = here()
    barrier = pltpu.get_barrier_semaphore()
    greet_line(barrier, x, z, k)
    pl.semaphore_wait(barrier, 4 * GRP - 1)

    def tile(ref, h):
        return ref.at[:, pl.ds(pl.multiple_of(h * HEAD_DIM, HEAD_DIM), HEAD_DIM)]

    grads = (gq, gk, gv)
    owner = lax.div(z, 2)
    side = lax.rem(z, 2)

    def each(i, begin):
        kind = lax.rem(x + i + z, 4)

        @pl.when(kind == 0)
        def _():
            for o in range(ROUNDS):
                own = jnp.logical_and(x == o, z == i)

                @pl.when(jnp.logical_not(own))
                def _(o=o):
                    cp = remote(rows.at[i], tile(att, z), ss.at[i, o], ra.at[z], device(o, i, k))
                    cp.start() if begin else cp.wait_send()

                @pl.when(own)
                def _():
                    local(tile(att, z), begin)

        for t in range(3):
            own = jnp.logical_and(x == owner, z == i)

            @pl.when(jnp.logical_and(kind == t + 1, jnp.logical_not(own)))
            def _(t=t):
                cp = remote(rows.at[i], tile(grads[t], side), ss.at[i, 0], rg.at[2 * t + side],
                            device(owner, i, k))
                cp.start() if begin else cp.wait_send()

            @pl.when(jnp.logical_and(kind == t + 1, own))
            def _(t=t):
                local(tile(grads[t], side), begin)

    def local(dst, begin):
        if begin:
            pltpu.make_async_copy(rows.at[z], buf, ls.at[0]).start()
            pltpu.make_async_copy(rows.at[z], buf, ls.at[0]).wait()
            pltpu.make_async_copy(buf, dst, ls.at[1]).start()
        else:
            pltpu.make_async_copy(buf, dst, ls.at[1]).wait()

    loop(0, GRP, lambda i: each(lax.rem(z + i, GRP), True))
    loop(0, GRP, lambda i: each(lax.rem(z + i, GRP), False))

    def arrive_att(h):
        sender = lax.rem(32 - z - h, 4)

        @pl.when(jnp.logical_not(jnp.logical_and(h == z, sender == x)))
        def _():
            remote(rows.at[0], tile(att, h), ss.at[0, 0], ra.at[h], device(sender, h, k)).wait_recv()

    loop(0, GRP, arrive_att)
    for t in range(3):
        for n in range(2):
            h = 2 * x + n
            sender = lax.rem(32 + t + 1 - z - h, 4)

            @pl.when(jnp.logical_not(jnp.logical_and(h == z, sender == x)))
            def _(t=t, n=n, h=h, sender=sender):
                remote(rows.at[0], tile(grads[t], n), ss.at[0, 0], rg.at[2 * t + n],
                       device(sender, h, k)).wait_recv()


def home(rows):
    dma = pltpu.SemaphoreType.DMA
    part = jax.ShapeDtypeStruct((TOK, 2 * HEAD_DIM), bf16)
    return pl.pallas_call(
        home_kernel,
        out_shape=(jax.ShapeDtypeStruct((TOK, HEADS * HEAD_DIM), bf16), part, part, part),
        in_specs=[pl.BlockSpec(memory_space=ANY)],
        out_specs=(pl.BlockSpec(memory_space=ANY),) * 4,
        scratch_shapes=[
            pltpu.VMEM((TOK, HEAD_DIM), bf16),
            dma((GRP, ROUNDS)), dma((GRP,)), dma((6,)), dma((2,)),
        ],
        compiler_params=pltpu.CompilerParams(collective_id=4, has_side_effects=True),
        name="home",
    )(rows)


def ranked(group, before):
    same = group[:, None] == group[None, :]
    return jnp.sum(jnp.logical_and(before, same).astype(i32), axis=1)


def shift(rows, step):
    n = lax.axis_size("seq")
    route = [(i, i - i % GRP + (i % GRP + step) % GRP) for i in range(n)]
    return lax.ppermute(rows, "seq", route)


def on_device(queries, keys, values, cotangent, order, inverse, bucket):
    s = lax.axis_index("seq")
    k = s % GRP
    z = s // GRP
    tokens = order[0]
    target = inverse[0] // TOK
    counter = jnp.arange(TOK, dtype=i32)
    sidx = target * SLOT + ranked(target, counter[None, :] < counter[:, None])
    source = tokens // TOK
    rank = ranked(source, tokens[None, :] < tokens[:, None])
    ridx = (source % GRP) * CHUNK + (source // GRP) * SLOT + rank
    zin, sall, rall = spread(queries, keys, values, cotangent,
                             sidx.reshape(1, TOK), ridx.reshape(1, TOK))
    place = jnp.arange(MSG, dtype=i32)
    mirror = (place // SLOT % GRP) * CHUNK + (place // CHUNK) * SLOT + place % SLOT
    swap = (mirror[:, None] == place[None, :]).astype(bf16)
    seq_len = bucket.shape[1]
    near = jnp.concatenate([bucket[0, -SPAN:], bucket[0]])
    bk = lax.dynamic_slice_in_dim(near, k * ROWS, ROWS + SPAN).astype(f32)
    bk = bk.reshape(NBLK + 1, 1, SPAN)
    recv = plane_exchange(pack_tokens(zin, sall), 1, "plane_out")
    rows = unpack_rows(recv, swap, rall)
    rows = rows.reshape(NBLK, SPAN, 4 * HEAD_DIM)
    tail = shift(rows[NBLK - 1, :, HEAD_DIM:3 * HEAD_DIM], 1)
    back = stats(forward(rows, tail, bk, swap, rall), sall)
    outq, outkv = backward(rows, tail, bk, back, swap, rall)
    spill = shift(outkv[0].astype(bf16), -1)
    packed = repack(z.reshape(1), outq, outkv, spill, swap, rall)
    settled = settle(plane_exchange(packed, 3, "plane_back"), sall)
    return home(settled)


def solution(mesh):
    return jax.shard_map(
        on_device,
        mesh=mesh,
        in_specs=(
            P("seq", None), P("seq", None), P("seq", None), P("seq", None),
            P("round", "seq"), P("round", "seq"), P("round", None),
        ),
        out_specs=(P("seq", None), P("seq", "round"), P("seq", "round"), P("seq", "round")),
        check_vma=False,
    )
```

```python
import jax
import jax.numpy as jnp
import numpy as np
from jax import lax
from jax.experimental import pallas as pl
from jax.experimental.pallas import tpu as pltpu
from jax.sharding import PartitionSpec as P

HEADS = 8
HEAD_DIM = 128
SPAN = 128
TOK = 256
SLOT = 6
GRP = 8
CHUNK = GRP * SLOT
MSG = GRP * CHUNK
ROUNDS = 4
ROWS = GRP * TOK
NBLK = ROWS // SPAN
NEG = -1e30
SCALE = HEAD_DIM ** (-0.5)
f32 = jnp.float32
bf16 = jnp.bfloat16
i32 = jnp.int32
ANY = pl.ANY


def here():
    x = lax.axis_index("round")
    s = lax.axis_index("seq")
    return x, lax.div(s, GRP), lax.rem(s, GRP)


def device(x, z, k):
    return {"seq": z * GRP + k, "round": x}


def remote(src, dst, send, recv, target):
    return pltpu.make_async_remote_copy(
        src_ref=src, dst_ref=dst, send_sem=send, recv_sem=recv,
        device_id=target, device_id_type=pl.DeviceIdType.MESH,
    )


def signal(sem, target):
    pl.semaphore_signal(sem, inc=1, device_id=target, device_id_type=pl.DeviceIdType.MESH)


def loop(lo, hi, body):
    def go(i, c):
        body(i)
        return c

    lax.fori_loop(lo, hi, go, 0)


def row_onehot(idx, count):
    places = lax.broadcasted_iota(i32, (count, TOK), 0)
    return jnp.where(places == idx, 1.0, 0.0).astype(bf16)


def col_of(idx):
    wide = jnp.broadcast_to(idx.astype(f32), (128, TOK))
    return jnp.concatenate([wide[:, :128].T, wide[:, 128:].T], axis=0).astype(i32)


def dot(a, b):
    return jnp.dot(a, b, preferred_element_type=f32)


def dot_nt(a, b):
    return lax.dot_general(a, b, (((1,), (1,)), ((), ())), preferred_element_type=f32)


def dot_tn(a, b):
    return lax.dot_general(a, b, (((0,), (0,)), ((), ())), preferred_element_type=f32)


def three(a):
    hi = a.astype(bf16)
    left = a - hi.astype(f32)
    mid = left.astype(bf16)
    low = (left - mid.astype(f32)).astype(bf16)
    return hi.astype(f32), mid.astype(f32), low.astype(f32)


def window(rows, tail, b):
    own = rows[b]
    if isinstance(b, int) and b == 0:
        before = tail[...]
    else:
        before = rows[b - 1][:, HEAD_DIM:3 * HEAD_DIM]
    keys = jnp.concatenate([before[:, :HEAD_DIM], own[:, HEAD_DIM:2 * HEAD_DIM]], axis=0)
    vals = jnp.concatenate([before[:, HEAD_DIM:], own[:, 2 * HEAD_DIM:3 * HEAD_DIM]], axis=0)
    return own[:, :HEAD_DIM], keys, vals, own[:, 3 * HEAD_DIM:]


def cols(ref, h):
    return ref.at[:, pl.ds(pl.multiple_of(h * HEAD_DIM, HEAD_DIM), HEAD_DIM)]


def both(copy):
    copy.wait_send()
    copy.wait_recv()


def ranks(col, row, before):
    return jnp.sum(jnp.where(jnp.logical_and(col == row, before), 1.0, 0.0), axis=0, keepdims=True)


def wide_col(row):
    col = col_of(row)
    return jnp.concatenate([col, col], axis=1)


def whole_kernel(
    q, k_, v, g_, inv, ordr, bucket, swap, final,
    sidx, ridx, sall, rall, zin, packed, recv, table, ohr, ohrt, ohst, mid, rows, tail,
    stat, smid, sent, got, across, reply, back, bmid, outq, outkv, spill_out, spill_in,
    packed2, recv2, settled, near,
    zs, zr, ss, sr, rs, rr, ls, ps, pr, ts, tr, s1, r1, s2, r2, s3, r3, ws, wr, bs, br, hs, hr,
):
    x, z, k = here()
    line = x * GRP + z
    me = x * GRP + k
    total = 4 * GRP
    barrier = pltpu.get_barrier_semaphore()

    def on_line(i):
        o = lax.rem(line + i, total)
        return o, device(lax.div(o, GRP), lax.rem(o, GRP), k)

    def on_plane(i):
        o = lax.rem(me + i * 11, total)
        return o, device(lax.div(o, GRP), z, lax.rem(o, GRP))

    def greet(i):
        signal(barrier, on_line(i)[1])
        signal(barrier, on_plane(i)[1])

    loop(1, total, greet)
    mine = (z == k).astype(i32)

    def greet_pos(i):
        @pl.when(jnp.logical_or(z != k, i != z))
        def _():
            signal(barrier, device(x, i, z))

        @pl.when(jnp.logical_or(z != k, i != k))
        def _():
            signal(barrier, device(x, k, i))

    loop(0, GRP, greet_pos)

    for t, ref in enumerate((q, k_, v, g_)):
        @pl.when(x == t)
        def _(ref=ref):
            pltpu.make_async_copy(cols(ref, z), zin.at[z], ls.at[0]).start()

    up = lax.broadcasted_iota(i32, (TOK, TOK), 0)
    across_ = lax.broadcasted_iota(i32, (TOK, TOK), 1)
    target = lax.shift_right_logical(inv[...], 8)
    rank = ranks(wide_col(target), target, up < across_).astype(i32)
    sidx[...] = target * SLOT + rank
    tokens = ordr[...]
    source = lax.shift_right_logical(tokens, 8)
    rank = ranks(wide_col(source), source, wide_col(tokens) < tokens).astype(i32)
    part = jnp.bitwise_and(source, GRP - 1)
    ridx[...] = part * CHUNK + lax.shift_right_logical(source, 3) * SLOT + rank

    pl.semaphore_wait(barrier, 2 * (total - 1) + 2 * (GRP - mine))

    def send_idx(i):
        o, target_ = on_line(i)
        remote(sidx, sall.at[line], ss.at[o], sr.at[line], target_).start()

    loop(1, total, send_idx)
    sall[line] = sidx[...]

    for t, ref in enumerate((q, k_, v, g_)):
        @pl.when(x == t)
        def _(ref=ref):
            def go(i):
                step = lax.div(i + 1, 2)
                o = lax.rem(z + jnp.where(lax.rem(i, 2) == 1, step, GRP - step), GRP)
                remote(cols(ref, o), zin.at[z], zs.at[o], zr.at[z], device(x, o, k)).start()

            loop(1, GRP, go)

    def send_pos(i):
        @pl.when(jnp.logical_or(z != k, i != z))
        def _():
            remote(ridx, rall.at[k], rs.at[i], rr.at[k], device(x, i, z)).start()

    loop(0, GRP, send_pos)

    @pl.when(z == k)
    def _():
        rall[k] = ridx[...]

    def wait_idx(i):
        o, target_ = on_line(i)
        both(remote(sidx, sall.at[o], ss.at[o], sr.at[o], target_))

    loop(1, total, wait_idx)

    def pack_one(i):
        @pl.when(i == z)
        def _():
            pltpu.make_async_copy(cols(q, z), zin.at[z], ls.at[0]).wait()

        @pl.when(i != z)
        def _():
            both(remote(cols(q, i), zin.at[i], zs.at[i], zr.at[i], device(x, i, k)))

        def per_round(r):
            onehot = row_onehot(sall[r * GRP + i], MSG)
            value = dot(onehot, zin[i]).astype(bf16).reshape(GRP, CHUNK, HEAD_DIM)
            packed[pl.ds(r * GRP, GRP), i] = value

        loop(0, ROUNDS, per_round)

    def pack_pair(j):
        p = lax.rem(lax.div(z, 2) + j + lax.div(j, 2) - 2 * lax.div(j, 3), 4)
        pack_one(2 * p)
        pack_one(2 * p + 1)

        def go(i):
            o, target_ = on_plane(i)
            remote(packed.at[o, pl.ds(2 * p, 2)], recv.at[me, pl.ds(2 * p, 2)],
                   ps.at[o, p], pr.at[me, p], target_).start()

        loop(1, total, go)

    loop(0, 4, pack_pair)
    recv[me] = packed[me]

    def wait_pos(i):
        @pl.when(jnp.logical_or(z != k, i != z))
        def _():
            remote(ridx, rall.at[k], rs.at[i], rr.at[i], device(x, i, z)).wait_send()

        @pl.when(jnp.logical_or(z != k, i != k))
        def _():
            remote(ridx, rall.at[i], rs.at[i], rr.at[i], device(x, k, i)).wait_recv()

    loop(0, GRP, wait_pos)

    lanes = lax.broadcasted_iota(i32, (TOK, 128), 1)

    def fill_near(b):
        near[b] = bucket[lax.rem(k * NBLK + b + GRP * NBLK - 1, GRP * NBLK)].astype(f32)

    loop(0, NBLK + 1, fill_near)

    def fill_pos(d):
        col = col_of(rall[d])
        for m in range(3):
            ohr[d, :, m * 128:(m + 1) * 128] = jnp.where(col == lanes + m * 128, 1.0, 0.0).astype(bf16)
        ohrt[d] = row_onehot(rall[d], MSG)

    loop(0, GRP, fill_pos)

    def fill_tok(n):
        col = col_of(sall[n])
        for m in range(3):
            ohst[n, :, m * 128:(m + 1) * 128] = jnp.where(col == lanes + m * 128, 1.0, 0.0).astype(bf16)

    loop(0, total, fill_tok)

    def fill_table(i):
        table[:, i] = row_onehot(sall[x * GRP + i], MSG).reshape(GRP, CHUNK, TOK)

    loop(0, GRP, fill_table)

    def first(i):
        g = lax.rem(k + i, GRP)

        def arrived(n):
            t = lax.div(n, 4)
            p = lax.rem(n, 4)
            o = t * GRP + g

            @pl.when(o != me)
            def _():
                both(remote(packed.at[o, pl.ds(2 * p, 2)], recv.at[o, pl.ds(2 * p, 2)],
                            ps.at[o, p], pr.at[o, p], device(t, z, g)))

        loop(0, 16, arrived)
        parts = [recv[t * GRP + g].reshape(MSG, HEAD_DIM) for t in range(4)]
        moved = dot(swap[...], jnp.concatenate(parts, axis=1)).astype(bf16)
        mid[:, g] = moved.reshape(GRP, CHUNK, 4 * HEAD_DIM)

    loop(0, GRP, first)

    def second(d):
        value = dot(ohr[d], mid[d].reshape(MSG, 4 * HEAD_DIM)).astype(bf16)
        rows[pl.ds(2 * d, 2)] = value.reshape(2, SPAN, 4 * HEAD_DIM)

    second(GRP - 1)
    after = device(x, z, lax.rem(k + 1, GRP))
    before = device(x, z, lax.rem(k + GRP - 1, GRP))
    tail_copy = remote(rows.at[NBLK - 1, :, pl.ds(HEAD_DIM, 2 * HEAD_DIM)], tail, ts.at[0], tr.at[0],
                       after)
    tail_copy.start()
    loop(0, GRP - 1, second)

    def allowed_of(b):
        own = near[b + 1]
        col = jnp.broadcast_to(own, (SPAN, SPAN)).T
        return jnp.concatenate([col == near[b], col == own], axis=1)

    lane8 = jnp.bitwise_and(lax.broadcasted_iota(i32, (SPAN, 128), 1), 7)

    def forward(b):
        query, keys, vals, grad = window(rows, tail, b)
        allowed = allowed_of(b)
        scores = jnp.where(allowed, dot_nt(query, keys) * SCALE, NEG)
        peak = jnp.max(scores, axis=-1, keepdims=True)
        expon = jnp.where(allowed, jnp.exp(scores - peak), 0.0)
        norm = jnp.sum(expon, axis=-1, keepdims=True)
        output = dot((expon / norm).astype(bf16), vals)
        lse = peak + jnp.log(norm)
        inner = jnp.sum(output * grad.astype(f32), axis=-1, keepdims=True)
        value = jnp.zeros((SPAN, 128), f32)
        for n, piece in enumerate(three(lse) + three(inner)):
            value = jnp.where(lane8 == n, piece, value)
        stat[b] = value.astype(bf16)

    loop(1, NBLK, forward)
    both(tail_copy)
    forward(0)
    group = lax.shift_right_logical(lax.broadcasted_iota(i32, (CHUNK, 128), 1), 3)

    def stat_pack(d):
        moved = dot(ohrt[d], stat[pl.ds(2 * d, 2)].reshape(TOK, 128))
        value = jnp.zeros((CHUNK, 128), f32)
        for g in range(GRP):
            value = jnp.where(group == g, moved[g * CHUNK:(g + 1) * CHUNK], value)
        smid[d] = value.astype(bf16)

    loop(0, GRP, stat_pack)
    sent[...] = dot(swap[...], smid[...].reshape(MSG, 128)).T[:8 * GRP].reshape(GRP, 8, MSG)

    def on_k(i):
        o = lax.rem(k + i, GRP)
        return o, device(x, z, o)

    def on_x(i):
        o = lax.rem(x + i, ROUNDS)
        return o, device(o, z, k)

    def go1(i):
        o, target_ = on_k(i)
        remote(sent.at[o], got.at[k], s1.at[o], r1.at[k], target_).start()

    loop(1, GRP, go1)
    got[k] = sent[k]

    def end1(i):
        o, target_ = on_k(i)
        both(remote(sent.at[o], got.at[o], s1.at[o], r1.at[o], target_))

    loop(1, GRP, end1)
    place = lax.broadcasted_iota(i32, (8, MSG), 1)
    start = lax.broadcasted_iota(i32, (8, MSG), 0) * CHUNK
    keep = jnp.logical_and(place >= start, place < start + CHUNK)

    def collect(o, acc):
        piece = got[o]
        wide = [jnp.where(keep, jnp.broadcast_to(piece[n:n + 1], (8, MSG)), 0.0) for n in range(6)]
        return acc + dot(jnp.concatenate(wide, axis=0).astype(bf16), table[o].reshape(MSG, TOK))

    tok = lax.fori_loop(0, GRP, collect, jnp.zeros((48, TOK), f32))
    across[x, 0] = tok[0:8] + tok[8:16] + tok[16:24]
    across[x, 1] = tok[24:32] + tok[32:40] + tok[40:48]

    def go2(i):
        o, target_ = on_x(i)
        remote(across.at[x], across.at[x], s2.at[o], r2.at[x], target_).start()

    loop(1, ROUNDS, go2)

    def end2(i):
        o, target_ = on_x(i)
        both(remote(across.at[x], across.at[o], s2.at[o], r2.at[o], target_))

    loop(1, ROUNDS, end2)
    lses = [across[r, 0] for r in range(ROUNDS)]
    top = jnp.maximum(jnp.maximum(lses[0], lses[1]), jnp.maximum(lses[2], lses[3]))
    exps = [jnp.exp(a - top) for a in lses]
    norm = (exps[0] + exps[1]) + (exps[2] + exps[3])
    joint = top + jnp.log(norm)
    delta = sum(exps[r] * across[r, 1] for r in range(ROUNDS)) / norm
    pieces = jnp.concatenate(three(joint) + three(delta), axis=0).astype(bf16)

    def answer(o):
        wide = dot_nt(pieces, table[o].reshape(MSG, TOK))
        parts = [jnp.sum(jnp.where(keep, wide[n * 8:(n + 1) * 8], 0.0), axis=0, keepdims=True)
                 for n in range(6)]
        parts += [jnp.zeros((2, MSG), f32)]
        reply[o] = jnp.concatenate(parts, axis=0)

    loop(0, GRP, answer)

    def go3(i):
        o, target_ = on_k(i)
        remote(reply.at[o], back.at[k], s3.at[o], r3.at[k], target_).start()

    loop(1, GRP, go3)
    back[k] = reply[k]

    def end3(i):
        o, target_ = on_k(i)
        both(remote(reply.at[o], back.at[o], s3.at[o], r3.at[o], target_))

    loop(1, GRP, end3)
    flat = jnp.concatenate(
        [back[...].reshape(8 * GRP, MSG), jnp.zeros((128 - 8 * GRP, MSG), f32)], axis=0
    )
    bmid[...] = dot(swap[...], flat.T.astype(bf16)).astype(bf16).reshape(GRP, CHUNK, 128)
    lane_tok = jnp.bitwise_and(lanes, 7)

    def joint_of(d):
        part_ = bmid[d].astype(f32)
        wide = jnp.concatenate(
            [jnp.where(group == g, part_, 0.0) for g in range(GRP)], axis=0
        ).astype(bf16)
        found = dot(ohr[d], wide)
        lse = jnp.sum(jnp.where(lane_tok < 3, found, 0.0), axis=-1, keepdims=True)
        dlt = jnp.sum(jnp.where(jnp.logical_and(lane_tok >= 3, lane_tok < 6), found, 0.0),
                      axis=-1, keepdims=True)
        return lse, dlt

    outkv[0] = jnp.zeros((SPAN, 2 * HEAD_DIM), f32)

    def backward(b, lse, dlt):
        query, keys, vals, grad = window(rows, tail, b)
        allowed = allowed_of(b)
        scores = dot_nt(query, keys) * SCALE
        prob = jnp.exp(jnp.where(allowed, scores - lse, NEG))
        low = prob.astype(bf16)
        value_grad = dot_tn(low, grad)
        prob_grad = dot_nt(grad, vals)
        score_grad = (prob * (prob_grad - dlt)).astype(bf16)
        query_grad = dot(score_grad, keys) * SCALE
        key_grad = dot_tn(score_grad, query) * SCALE
        outq[b] = jnp.concatenate([dot(low, vals), query_grad], axis=1).astype(bf16)
        pair = jnp.concatenate([key_grad, value_grad], axis=1)
        outkv[b] = outkv[b] + pair[:SPAN]
        outkv[b + 1] = pair[SPAN:]

    def backward_pair(d):
        lse, dlt = joint_of(d)
        backward(2 * d, lse[:SPAN], dlt[:SPAN])
        backward(2 * d + 1, lse[SPAN:], dlt[SPAN:])

    backward_pair(0)
    spill_out[...] = outkv[0].astype(bf16)
    spill_copy = remote(spill_out, spill_in, ws.at[0], wr.at[0], before)
    spill_copy.start()
    loop(1, GRP, backward_pair)

    def repack(d):
        upper = jnp.concatenate([outq[2 * d], outkv[2 * d + 1].astype(bf16)], axis=1)
        lower = jnp.concatenate([outq[2 * d + 1], outkv[2 * d + 2].astype(bf16)], axis=1)
        moved = dot(ohrt[d], jnp.concatenate([upper, lower], axis=0)).astype(bf16)
        mid[:, d] = moved.reshape(GRP, CHUNK, 4 * HEAD_DIM)

    loop(0, GRP - 1, repack)
    both(spill_copy)
    outkv[NBLK] = outkv[NBLK] + spill_in[...].astype(f32)
    repack(GRP - 1)

    def reorder(g):
        moved = dot(swap[...], mid[g].reshape(MSG, 4 * HEAD_DIM)).astype(bf16)
        for i in range(GRP):
            for t in range(4):
                owner = lax.rem(t - i - z + 16, 4)
                packed2[owner * GRP + g, i] = moved[i * CHUNK:(i + 1) * CHUNK,
                                                    t * HEAD_DIM:(t + 1) * HEAD_DIM]

    loop(0, GRP, reorder)

    def back_pair(j):
        p = lax.rem(lax.div(z, 2) + j, 4)

        def go(i):
            o, target_ = on_plane(i)
            remote(packed2.at[o, pl.ds(2 * p, 2)], recv2.at[me, pl.ds(2 * p, 2)],
                   bs.at[o, p], br.at[me, p], target_).start()

        loop(1, total, go)

    loop(0, 4, back_pair)
    recv2[me] = packed2[me]
    owner = lax.div(z, 2)
    side = lax.rem(z, 2)

    def home(i, begin):
        kind = lax.rem(x + i + z, 4)

        @pl.when(kind == 0)
        def _():
            for o in range(ROUNDS):
                own = jnp.logical_and(x == o, z == i)

                @pl.when(jnp.logical_not(own))
                def _(o=o):
                    cp = remote(settled.at[i], final.at[z], hs.at[i, o], hr.at[z], device(o, i, k))
                    cp.start() if begin else cp.wait_send()

                @pl.when(own)
                def _():
                    cp = pltpu.make_async_copy(settled.at[i], final.at[z], ls.at[1])
                    cp.start() if begin else cp.wait()

        tile = GRP + 2 * (kind - 1) + side
        own = jnp.logical_and(x == owner, z == i)

        @pl.when(jnp.logical_and(kind != 0, jnp.logical_not(own)))
        def _():
            cp = remote(settled.at[i], final.at[tile], hs.at[i, 0], hr.at[tile], device(owner, i, k))
            cp.start() if begin else cp.wait_send()

        @pl.when(jnp.logical_and(kind != 0, own))
        def _():
            cp = pltpu.make_async_copy(settled.at[i], final.at[tile], ls.at[1])
            cp.start() if begin else cp.wait()

    def settle(i):
        acc = jnp.zeros((TOK, HEAD_DIM), f32)
        for r in range(ROUNDS):
            acc = acc + dot(ohst[r * GRP + i], recv2[r * GRP:(r + 1) * GRP, i].reshape(MSG, HEAD_DIM))
        settled[i] = acc.astype(bf16)
        home(i, True)

    def settle_pair(j):
        p = lax.rem(lax.div(z, 2) + j, 4)

        def end(i):
            o, target_ = on_plane(i)
            both(remote(packed2.at[o, pl.ds(2 * p, 2)], recv2.at[o, pl.ds(2 * p, 2)],
                        bs.at[o, p], br.at[o, p], target_))

        loop(1, total, end)
        loop(2 * p, 2 * p + 2, settle)

    loop(0, 4, settle_pair)
    loop(0, GRP, lambda i: home(i, False))

    def arrive(tile, kind, h):
        sender = lax.rem(32 + kind - z - h, 4)

        @pl.when(jnp.logical_not(jnp.logical_and(h == z, sender == x)))
        def _():
            remote(settled.at[0], final.at[tile], hs.at[0, 0], hr.at[tile],
                   device(sender, h, k)).wait_recv()

    loop(0, GRP, lambda h: arrive(h, 0, h))
    loop(0, 6, lambda n: arrive(GRP + n, 1 + lax.div(n, 2), 2 * x + lax.rem(n, 2)))


def whole(q, k, v, g, inv, ordr, bucket, swap):
    n = 4 * GRP
    dma = pltpu.SemaphoreType.DMA
    vm = pltpu.VMEM
    spec = pl.BlockSpec(memory_space=pltpu.VMEM)
    wide = 4 * HEAD_DIM
    return pl.pallas_call(
        whole_kernel,
        out_shape=jax.ShapeDtypeStruct((14, TOK, HEAD_DIM), bf16),
        in_specs=[pl.BlockSpec(memory_space=ANY)] * 4 + [spec] * 4,
        out_specs=pl.BlockSpec(memory_space=ANY),
        scratch_shapes=[
            vm((1, TOK), i32), vm((1, TOK), i32), vm((n, 1, TOK), i32), vm((GRP, 1, TOK), i32),
            vm((GRP, TOK, HEAD_DIM), bf16),
            vm((n, GRP, CHUNK, HEAD_DIM), bf16), vm((n, GRP, CHUNK, HEAD_DIM), bf16),
            vm((GRP, GRP, CHUNK, TOK), bf16), vm((GRP, TOK, MSG), bf16), vm((GRP, MSG, TOK), bf16),
            vm((n, TOK, MSG), bf16), vm((GRP, GRP, CHUNK, wide), bf16),
            vm((NBLK, SPAN, wide), bf16), vm((SPAN, 2 * HEAD_DIM), bf16),
            vm((NBLK, SPAN, 128), bf16), vm((GRP, CHUNK, 128), bf16),
            vm((GRP, 8, MSG), f32), vm((GRP, 8, MSG), f32), vm((ROUNDS, 2, GRP, TOK), f32),
            vm((GRP, 8, MSG), f32), vm((GRP, 8, MSG), f32), vm((GRP, CHUNK, 128), bf16),
            vm((NBLK, SPAN, 2 * HEAD_DIM), bf16), vm((NBLK + 1, SPAN, 2 * HEAD_DIM), f32),
            vm((SPAN, 2 * HEAD_DIM), bf16), vm((SPAN, 2 * HEAD_DIM), bf16),
            vm((n, GRP, CHUNK, HEAD_DIM), bf16), vm((n, GRP, CHUNK, HEAD_DIM), bf16),
            vm((GRP, TOK, HEAD_DIM), bf16), vm((NBLK + 1, 1, SPAN), f32),
            dma((GRP,)), dma((GRP,)), dma((n,)), dma((n,)), dma((GRP,)), dma((GRP,)), dma((2,)),
            dma((n, 4)), dma((n, 4)), dma((1,)), dma((1,)),
            dma((GRP,)), dma((GRP,)), dma((ROUNDS,)), dma((ROUNDS,)), dma((GRP,)), dma((GRP,)),
            dma((1,)), dma((1,)), dma((n, 4)), dma((n, 4)), dma((GRP, ROUNDS)), dma((14,)),
        ],
        compiler_params=pltpu.CompilerParams(
            collective_id=0, has_side_effects=True, vmem_limit_bytes=60 * 1024 * 1024
        ),
        name="whole",
    )(q, k, v, g, inv, ordr, bucket, swap)


def finish_kernel(tiles, att, gq, gk, gv):
    for h in range(HEADS):
        att[:, h * HEAD_DIM:(h + 1) * HEAD_DIM] = tiles[h]
    for t, ref in enumerate((gq, gk, gv)):
        for n in range(2):
            ref[:, n * HEAD_DIM:(n + 1) * HEAD_DIM] = tiles[GRP + 2 * t + n]


def finish(tiles):
    part = jax.ShapeDtypeStruct((TOK, 2 * HEAD_DIM), bf16)
    return pl.pallas_call(
        finish_kernel,
        out_shape=(jax.ShapeDtypeStruct((TOK, HEADS * HEAD_DIM), bf16), part, part, part),
        name="finish",
    )(tiles)


def swap_matrix():
    at = np.arange(MSG)
    mirror = (at // SLOT % GRP) * CHUNK + (at // CHUNK) * SLOT + at % SLOT
    return (mirror[:, None] == at[None, :]).astype(jnp.bfloat16)


def on_device(queries, keys, values, cotangent, order, inverse, bucket):
    return finish(whole(queries, keys, values, cotangent, inverse, order,
                        bucket.reshape(GRP * NBLK, 1, SPAN), jnp.asarray(swap_matrix())))


def solution(mesh):
    return jax.shard_map(
        on_device,
        mesh=mesh,
        in_specs=(
            P("seq", None), P("seq", None), P("seq", None), P("seq", None),
            P("round", "seq"), P("round", "seq"), P("round", None),
        ),
        out_specs=(P("seq", None), P("seq", "round"), P("seq", "round"), P("seq", "round")),
        check_vma=False,
    )
```

```python
import jax
import jax.numpy as jnp
import numpy as np
from jax import lax
from jax.experimental import pallas as pl
from jax.experimental.pallas import tpu as pltpu
from jax.sharding import PartitionSpec as P

HEADS = 8
HEAD_DIM = 128
SPAN = 128
TOK = 256
SLOT = 6
GRP = 8
CHUNK = GRP * SLOT
MSG = GRP * CHUNK
ROUNDS = 4
ROWS = GRP * TOK
NBLK = ROWS // SPAN
NEG = -1e30
SCALE = HEAD_DIM ** (-0.5)
f32 = jnp.float32
bf16 = jnp.bfloat16
i32 = jnp.int32
ANY = pl.ANY


def here():
    x = lax.axis_index("round")
    s = lax.axis_index("seq")
    return x, lax.div(s, GRP), lax.rem(s, GRP)


def device(x, z, k):
    return {"seq": z * GRP + k, "round": x}


def remote(src, dst, send, recv, target):
    return pltpu.make_async_remote_copy(
        src_ref=src, dst_ref=dst, send_sem=send, recv_sem=recv,
        device_id=target, device_id_type=pl.DeviceIdType.MESH,
    )


def signal(sem, target):
    pl.semaphore_signal(sem, inc=1, device_id=target, device_id_type=pl.DeviceIdType.MESH)


def loop(lo, hi, body):
    def go(i, c):
        body(i)
        return c

    lax.fori_loop(lo, hi, go, 0)


def row_onehot(idx, count):
    places = lax.broadcasted_iota(i32, (count, TOK), 0)
    return jnp.where(places == idx, 1.0, 0.0).astype(bf16)


def col_of(idx):
    wide = jnp.broadcast_to(idx.astype(f32), (128, TOK))
    return jnp.concatenate([wide[:, :128].T, wide[:, 128:].T], axis=0).astype(i32)


def dot(a, b):
    return jnp.dot(a, b, preferred_element_type=f32)


def dot_nt(a, b):
    return lax.dot_general(a, b, (((1,), (1,)), ((), ())), preferred_element_type=f32)


def dot_tn(a, b):
    return lax.dot_general(a, b, (((0,), (0,)), ((), ())), preferred_element_type=f32)


def three(a):
    hi = a.astype(bf16)
    left = a - hi.astype(f32)
    mid = left.astype(bf16)
    low = (left - mid.astype(f32)).astype(bf16)
    return hi.astype(f32), mid.astype(f32), low.astype(f32)


def window(rows, tail, b):
    own = rows[b]
    if isinstance(b, int) and b == 0:
        before = tail[...]
    else:
        before = rows[b - 1][:, HEAD_DIM:3 * HEAD_DIM]
    keys = jnp.concatenate([before[:, :HEAD_DIM], own[:, HEAD_DIM:2 * HEAD_DIM]], axis=0)
    vals = jnp.concatenate([before[:, HEAD_DIM:], own[:, 2 * HEAD_DIM:3 * HEAD_DIM]], axis=0)
    return own[:, :HEAD_DIM], keys, vals, own[:, 3 * HEAD_DIM:]


def cols(ref, h):
    return ref.at[:, pl.ds(pl.multiple_of(h * HEAD_DIM, HEAD_DIM), HEAD_DIM)]


def both(copy):
    copy.wait_send()
    copy.wait_recv()


def ranks(col, row, before):
    return jnp.sum(jnp.where(jnp.logical_and(col == row, before), 1.0, 0.0), axis=0, keepdims=True)


def wide_col(row):
    col = col_of(row)
    return jnp.concatenate([col, col], axis=1)


def whole_kernel(
    q, k_, v, g_, inv, ordr, bucket, swap, final,
    sidx, ridx, sall, rall, zin, packed, recv, table, ohr, ohrt, ohst, mid, rows, tail,
    stat, smid, sent, got, across, reply, back, bmid, outq, outkv, spill_out, spill_in,
    packed2, recv2, settled, near, score, pgrad,
    zs, zr, ss, sr, rs, rr, ls, ps, pr, ts, tr, s1, r1, s2, r2, s3, r3, ws, wr, bs, br, hs, hr,
):
    x, z, k = here()
    line = x * GRP + z
    me = x * GRP + k
    total = 4 * GRP
    barrier = pltpu.get_barrier_semaphore()

    def on_line(i):
        o = lax.rem(line + i, total)
        return o, device(lax.div(o, GRP), lax.rem(o, GRP), k)

    def on_plane(i):
        o = lax.rem(me + i * 11, total)
        return o, device(lax.div(o, GRP), z, lax.rem(o, GRP))

    def greet(i):
        signal(barrier, on_line(i)[1])
        signal(barrier, on_plane(i)[1])

    loop(1, total, greet)
    mine = (z == k).astype(i32)

    def greet_pos(i):
        @pl.when(jnp.logical_or(z != k, i != z))
        def _():
            signal(barrier, device(x, i, z))

        @pl.when(jnp.logical_or(z != k, i != k))
        def _():
            signal(barrier, device(x, k, i))

    loop(0, GRP, greet_pos)

    for t, ref in enumerate((q, k_, v, g_)):
        @pl.when(x == t)
        def _(ref=ref):
            pltpu.make_async_copy(cols(ref, z), zin.at[z], ls.at[0]).start()

    up = lax.broadcasted_iota(i32, (TOK, TOK), 0)
    across_ = lax.broadcasted_iota(i32, (TOK, TOK), 1)
    target = lax.shift_right_logical(inv[...], 8)
    rank = ranks(wide_col(target), target, up < across_).astype(i32)
    sidx[...] = target * SLOT + rank
    tokens = ordr[...]
    source = lax.shift_right_logical(tokens, 8)
    rank = ranks(wide_col(source), source, wide_col(tokens) < tokens).astype(i32)
    part = jnp.bitwise_and(source, GRP - 1)
    ridx[...] = part * CHUNK + lax.shift_right_logical(source, 3) * SLOT + rank

    pl.semaphore_wait(barrier, 2 * (total - 1) + 2 * (GRP - mine))

    def send_idx(i):
        o, target_ = on_line(i)
        remote(sidx, sall.at[line], ss.at[o], sr.at[line], target_).start()

    loop(1, total, send_idx)
    sall[line] = sidx[...]

    for t, ref in enumerate((q, k_, v, g_)):
        @pl.when(x == t)
        def _(ref=ref):
            def go(i):
                step = lax.div(i + 1, 2)
                o = lax.rem(z + jnp.where(lax.rem(i, 2) == 1, step, GRP - step), GRP)
                remote(cols(ref, o), zin.at[z], zs.at[o], zr.at[z], device(x, o, k)).start()

            loop(1, GRP, go)

    def send_pos(i):
        @pl.when(jnp.logical_or(z != k, i != z))
        def _():
            remote(ridx, rall.at[k], rs.at[i], rr.at[k], device(x, i, z)).start()

    loop(0, GRP, send_pos)

    @pl.when(z == k)
    def _():
        rall[k] = ridx[...]

    def wait_idx(i):
        o, target_ = on_line(i)
        both(remote(sidx, sall.at[o], ss.at[o], sr.at[o], target_))

    loop(1, total, wait_idx)

    def pack_one(i):
        @pl.when(i == z)
        def _():
            pltpu.make_async_copy(cols(q, z), zin.at[z], ls.at[0]).wait()

        @pl.when(i != z)
        def _():
            both(remote(cols(q, i), zin.at[i], zs.at[i], zr.at[i], device(x, i, k)))

        def per_round(r):
            onehot = row_onehot(sall[r * GRP + i], MSG)
            value = dot(onehot, zin[i]).astype(bf16).reshape(GRP, CHUNK, HEAD_DIM)
            packed[pl.ds(r * GRP, GRP), i] = value

        loop(0, ROUNDS, per_round)

    def pack_pair(j):
        p = lax.rem(lax.div(z, 2) + j + lax.div(j, 2) - 2 * lax.div(j, 3), 4)
        pack_one(2 * p)
        pack_one(2 * p + 1)

        def go(i):
            o, target_ = on_plane(i)
            remote(packed.at[o, pl.ds(2 * p, 2)], recv.at[me, pl.ds(2 * p, 2)],
                   ps.at[o, p], pr.at[me, p], target_).start()

        loop(1, total, go)

    loop(0, 4, pack_pair)
    recv[me] = packed[me]

    def wait_pos(i):
        @pl.when(jnp.logical_or(z != k, i != z))
        def _():
            remote(ridx, rall.at[k], rs.at[i], rr.at[i], device(x, i, z)).wait_send()

        @pl.when(jnp.logical_or(z != k, i != k))
        def _():
            remote(ridx, rall.at[i], rs.at[i], rr.at[i], device(x, k, i)).wait_recv()

    loop(0, GRP, wait_pos)

    lanes = lax.broadcasted_iota(i32, (TOK, 128), 1)

    def fill_near(b):
        near[b] = bucket[lax.rem(k * NBLK + b + GRP * NBLK - 1, GRP * NBLK)].astype(f32)

    loop(0, NBLK + 1, fill_near)

    def fill_pos(d):
        col = col_of(rall[d])
        for m in range(3):
            ohr[d, :, m * 128:(m + 1) * 128] = jnp.where(col == lanes + m * 128, 1.0, 0.0).astype(bf16)
        ohrt[d] = row_onehot(rall[d], MSG)

    loop(0, GRP, fill_pos)

    def fill_tok(n):
        col = col_of(sall[n])
        for m in range(3):
            ohst[n, :, m * 128:(m + 1) * 128] = jnp.where(col == lanes + m * 128, 1.0, 0.0).astype(bf16)

    loop(0, total, fill_tok)

    def fill_table(i):
        table[:, i] = row_onehot(sall[x * GRP + i], MSG).reshape(GRP, CHUNK, TOK)

    loop(0, GRP, fill_table)

    def first(i):
        g = lax.rem(k + i, GRP)

        def arrived(n):
            t = lax.div(n, 4)
            p = lax.rem(n, 4)
            o = t * GRP + g

            @pl.when(o != me)
            def _():
                both(remote(packed.at[o, pl.ds(2 * p, 2)], recv.at[o, pl.ds(2 * p, 2)],
                            ps.at[o, p], pr.at[o, p], device(t, z, g)))

        loop(0, 16, arrived)
        parts = [recv[t * GRP + g].reshape(MSG, HEAD_DIM) for t in range(4)]
        moved = dot(swap[...], jnp.concatenate(parts, axis=1)).astype(bf16)
        mid[:, g] = moved.reshape(GRP, CHUNK, 4 * HEAD_DIM)

    loop(0, GRP, first)

    def second(d):
        value = dot(ohr[d], mid[d].reshape(MSG, 4 * HEAD_DIM)).astype(bf16)
        rows[pl.ds(2 * d, 2)] = value.reshape(2, SPAN, 4 * HEAD_DIM)

    second(GRP - 1)
    after = device(x, z, lax.rem(k + 1, GRP))
    before = device(x, z, lax.rem(k + GRP - 1, GRP))
    tail_copy = remote(rows.at[NBLK - 1, :, pl.ds(HEAD_DIM, 2 * HEAD_DIM)], tail, ts.at[0], tr.at[0],
                       after)
    tail_copy.start()
    loop(0, GRP - 1, second)

    def allowed_of(b):
        own = near[b + 1]
        col = jnp.broadcast_to(own, (SPAN, SPAN)).T
        return jnp.concatenate([col == near[b], col == own], axis=1)

    lane8 = jnp.bitwise_and(lax.broadcasted_iota(i32, (SPAN, 128), 1), 7)

    def forward(b):
        query, keys, vals, grad = window(rows, tail, b)
        allowed = allowed_of(b)
        scores = jnp.where(allowed, dot_nt(query, keys) * SCALE, NEG)
        score[b] = scores
        peak = jnp.max(scores, axis=-1, keepdims=True)
        expon = jnp.where(allowed, jnp.exp(scores - peak), 0.0)
        norm = jnp.sum(expon, axis=-1, keepdims=True)
        output = dot((expon / norm).astype(bf16), vals)
        lse = peak + jnp.log(norm)
        inner = jnp.sum(output * grad.astype(f32), axis=-1, keepdims=True)
        value = jnp.zeros((SPAN, 128), f32)
        for n, piece in enumerate(three(lse) + three(inner)):
            value = jnp.where(lane8 == n, piece, value)
        stat[b] = value.astype(bf16)

    def forward_three(j):
        for n in range(3):
            forward(1 + 3 * j + n)

    loop(0, 5, forward_three)
    both(tail_copy)
    forward(0)
    group = lax.shift_right_logical(lax.broadcasted_iota(i32, (CHUNK, 128), 1), 3)

    def stat_pack(d):
        moved = dot(ohrt[d], stat[pl.ds(2 * d, 2)].reshape(TOK, 128))
        value = jnp.zeros((CHUNK, 128), f32)
        for g in range(GRP):
            value = jnp.where(group == g, moved[g * CHUNK:(g + 1) * CHUNK], value)
        smid[d] = value.astype(bf16)

    loop(0, GRP, stat_pack)
    sent[...] = dot(swap[...], smid[...].reshape(MSG, 128)).T[:8 * GRP].reshape(GRP, 8, MSG)

    def on_k(i):
        o = lax.rem(k + i, GRP)
        return o, device(x, z, o)

    def on_x(i):
        o = lax.rem(x + i, ROUNDS)
        return o, device(o, z, k)

    def go1(i):
        o, target_ = on_k(i)
        remote(sent.at[o], got.at[k], s1.at[o], r1.at[k], target_).start()

    loop(1, GRP, go1)
    got[k] = sent[k]

    def prob_grad_of(b):
        _, _, vals, grad = window(rows, tail, b)
        pgrad[b] = dot_nt(grad, vals)

    def prob_grad_three(j):
        for n in range(3):
            prob_grad_of(1 + 3 * j + n)

    prob_grad_of(0)
    loop(0, 5, prob_grad_three)

    def end1(i):
        o, target_ = on_k(i)
        both(remote(sent.at[o], got.at[o], s1.at[o], r1.at[o], target_))

    loop(1, GRP, end1)
    place = lax.broadcasted_iota(i32, (8, MSG), 1)
    start = lax.broadcasted_iota(i32, (8, MSG), 0) * CHUNK
    keep = jnp.logical_and(place >= start, place < start + CHUNK)

    def collect(o, acc):
        piece = got[o]
        wide = [jnp.where(keep, jnp.broadcast_to(piece[n:n + 1], (8, MSG)), 0.0) for n in range(6)]
        return acc + dot(jnp.concatenate(wide, axis=0).astype(bf16), table[o].reshape(MSG, TOK))

    tok = lax.fori_loop(0, GRP, collect, jnp.zeros((48, TOK), f32))
    across[x, 0] = tok[0:8] + tok[8:16] + tok[16:24]
    across[x, 1] = tok[24:32] + tok[32:40] + tok[40:48]

    def go2(i):
        o, target_ = on_x(i)
        remote(across.at[x], across.at[x], s2.at[o], r2.at[x], target_).start()

    loop(1, ROUNDS, go2)

    def end2(i):
        o, target_ = on_x(i)
        both(remote(across.at[x], across.at[o], s2.at[o], r2.at[o], target_))

    loop(1, ROUNDS, end2)
    lses = [across[r, 0] for r in range(ROUNDS)]
    top = jnp.maximum(jnp.maximum(lses[0], lses[1]), jnp.maximum(lses[2], lses[3]))
    exps = [jnp.exp(a - top) for a in lses]
    norm = (exps[0] + exps[1]) + (exps[2] + exps[3])
    joint = top + jnp.log(norm)
    delta = sum(exps[r] * across[r, 1] for r in range(ROUNDS)) / norm
    pieces = jnp.concatenate(three(joint) + three(delta), axis=0).astype(bf16)

    def answer(o):
        wide = dot_nt(pieces, table[o].reshape(MSG, TOK))
        parts = [jnp.sum(jnp.where(keep, wide[n * 8:(n + 1) * 8], 0.0), axis=0, keepdims=True)
                 for n in range(6)]
        parts += [jnp.zeros((2, MSG), f32)]
        reply[o] = jnp.concatenate(parts, axis=0)

    loop(0, GRP, answer)

    def go3(i):
        o, target_ = on_k(i)
        remote(reply.at[o], back.at[k], s3.at[o], r3.at[k], target_).start()

    loop(1, GRP, go3)
    back[k] = reply[k]

    def end3(i):
        o, target_ = on_k(i)
        both(remote(reply.at[o], back.at[o], s3.at[o], r3.at[o], target_))

    loop(1, GRP, end3)
    flat = jnp.concatenate(
        [back[...].reshape(8 * GRP, MSG), jnp.zeros((128 - 8 * GRP, MSG), f32)], axis=0
    )
    bmid[...] = dot(swap[...], flat.T.astype(bf16)).astype(bf16).reshape(GRP, CHUNK, 128)
    lane_tok = jnp.bitwise_and(lanes, 7)

    def joint_of(d):
        part_ = bmid[d].astype(f32)
        wide = jnp.concatenate(
            [jnp.where(group == g, part_, 0.0) for g in range(GRP)], axis=0
        ).astype(bf16)
        found = dot(ohr[d], wide)
        lse = jnp.sum(jnp.where(lane_tok < 3, found, 0.0), axis=-1, keepdims=True)
        dlt = jnp.sum(jnp.where(jnp.logical_and(lane_tok >= 3, lane_tok < 6), found, 0.0),
                      axis=-1, keepdims=True)
        return lse, dlt

    outkv[0] = jnp.zeros((SPAN, 2 * HEAD_DIM), f32)

    def backward(b, lse, dlt):
        query, keys, vals, grad = window(rows, tail, b)
        prob = jnp.exp(score[b] - lse)
        low = prob.astype(bf16)
        value_grad = dot_tn(low, grad)
        score_grad = (prob * (pgrad[b] - dlt)).astype(bf16)
        query_grad = dot(score_grad, keys) * SCALE
        key_grad = dot_tn(score_grad, query) * SCALE
        outq[b] = jnp.concatenate([dot(low, vals), query_grad], axis=1).astype(bf16)
        pair = jnp.concatenate([key_grad, value_grad], axis=1)
        outkv[b] = outkv[b] + pair[:SPAN]
        outkv[b + 1] = pair[SPAN:]

    def backward_pair(d):
        lse, dlt = joint_of(d)
        backward(2 * d, lse[:SPAN], dlt[:SPAN])
        backward(2 * d + 1, lse[SPAN:], dlt[SPAN:])

    backward_pair(0)
    spill_out[...] = outkv[0].astype(bf16)
    spill_copy = remote(spill_out, spill_in, ws.at[0], wr.at[0], before)
    spill_copy.start()
    loop(1, GRP, backward_pair)

    def repack(d):
        upper = jnp.concatenate([outq[2 * d], outkv[2 * d + 1].astype(bf16)], axis=1)
        lower = jnp.concatenate([outq[2 * d + 1], outkv[2 * d + 2].astype(bf16)], axis=1)
        moved = dot(ohrt[d], jnp.concatenate([upper, lower], axis=0)).astype(bf16)
        mid[:, d] = moved.reshape(GRP, CHUNK, 4 * HEAD_DIM)

    loop(0, GRP - 1, repack)
    both(spill_copy)
    outkv[NBLK] = outkv[NBLK] + spill_in[...].astype(f32)
    repack(GRP - 1)

    def reorder(g):
        moved = dot(swap[...], mid[g].reshape(MSG, 4 * HEAD_DIM)).astype(bf16)
        for i in range(GRP):
            for t in range(4):
                owner = lax.rem(t - i - z + 16, 4)
                packed2[owner * GRP + g, i] = moved[i * CHUNK:(i + 1) * CHUNK,
                                                    t * HEAD_DIM:(t + 1) * HEAD_DIM]

    loop(0, GRP, reorder)

    def back_pair(j):
        p = lax.rem(lax.div(z, 2) + j, 4)

        def go(i):
            o, target_ = on_plane(i)
            remote(packed2.at[o, pl.ds(2 * p, 2)], recv2.at[me, pl.ds(2 * p, 2)],
                   bs.at[o, p], br.at[me, p], target_).start()

        loop(1, total, go)

    loop(0, 4, back_pair)
    recv2[me] = packed2[me]
    owner = lax.div(z, 2)
    side = lax.rem(z, 2)

    def home(i, begin):
        kind = lax.rem(x + i + z, 4)

        @pl.when(kind == 0)
        def _():
            for o in range(ROUNDS):
                own = jnp.logical_and(x == o, z == i)

                @pl.when(jnp.logical_not(own))
                def _(o=o):
                    cp = remote(settled.at[i], final.at[z], hs.at[i, o], hr.at[z], device(o, i, k))
                    cp.start() if begin else cp.wait_send()

                @pl.when(own)
                def _():
                    cp = pltpu.make_async_copy(settled.at[i], final.at[z], ls.at[1])
                    cp.start() if begin else cp.wait()

        tile = GRP + 2 * (kind - 1) + side
        own = jnp.logical_and(x == owner, z == i)

        @pl.when(jnp.logical_and(kind != 0, jnp.logical_not(own)))
        def _():
            cp = remote(settled.at[i], final.at[tile], hs.at[i, 0], hr.at[tile], device(owner, i, k))
            cp.start() if begin else cp.wait_send()

        @pl.when(jnp.logical_and(kind != 0, own))
        def _():
            cp = pltpu.make_async_copy(settled.at[i], final.at[tile], ls.at[1])
            cp.start() if begin else cp.wait()

    def settle(i):
        acc = jnp.zeros((TOK, HEAD_DIM), f32)
        for r in range(ROUNDS):
            acc = acc + dot(ohst[r * GRP + i], recv2[r * GRP:(r + 1) * GRP, i].reshape(MSG, HEAD_DIM))
        settled[i] = acc.astype(bf16)
        home(i, True)

    def settle_pair(j):
        p = lax.rem(lax.div(z, 2) + j, 4)

        def end(i):
            o, target_ = on_plane(i)
            both(remote(packed2.at[o, pl.ds(2 * p, 2)], recv2.at[o, pl.ds(2 * p, 2)],
                        bs.at[o, p], br.at[o, p], target_))

        loop(1, total, end)
        loop(2 * p, 2 * p + 2, settle)

    loop(0, 4, settle_pair)
    loop(0, GRP, lambda i: home(i, False))

    def arrive(tile, kind, h):
        sender = lax.rem(32 + kind - z - h, 4)

        @pl.when(jnp.logical_not(jnp.logical_and(h == z, sender == x)))
        def _():
            remote(settled.at[0], final.at[tile], hs.at[0, 0], hr.at[tile],
                   device(sender, h, k)).wait_recv()

    loop(0, GRP, lambda h: arrive(h, 0, h))
    loop(0, 6, lambda n: arrive(GRP + n, 1 + lax.div(n, 2), 2 * x + lax.rem(n, 2)))


def whole(q, k, v, g, inv, ordr, bucket, swap):
    n = 4 * GRP
    dma = pltpu.SemaphoreType.DMA
    vm = pltpu.VMEM
    spec = pl.BlockSpec(memory_space=pltpu.VMEM)
    wide = 4 * HEAD_DIM
    return pl.pallas_call(
        whole_kernel,
        out_shape=jax.ShapeDtypeStruct((14, TOK, HEAD_DIM), bf16),
        in_specs=[pl.BlockSpec(memory_space=ANY)] * 4 + [spec] * 4,
        out_specs=pl.BlockSpec(memory_space=ANY),
        scratch_shapes=[
            vm((1, TOK), i32), vm((1, TOK), i32), vm((n, 1, TOK), i32), vm((GRP, 1, TOK), i32),
            vm((GRP, TOK, HEAD_DIM), bf16),
            vm((n, GRP, CHUNK, HEAD_DIM), bf16), vm((n, GRP, CHUNK, HEAD_DIM), bf16),
            vm((GRP, GRP, CHUNK, TOK), bf16), vm((GRP, TOK, MSG), bf16), vm((GRP, MSG, TOK), bf16),
            vm((n, TOK, MSG), bf16), vm((GRP, GRP, CHUNK, wide), bf16),
            vm((NBLK, SPAN, wide), bf16), vm((SPAN, 2 * HEAD_DIM), bf16),
            vm((NBLK, SPAN, 128), bf16), vm((GRP, CHUNK, 128), bf16),
            vm((GRP, 8, MSG), f32), vm((GRP, 8, MSG), f32), vm((ROUNDS, 2, GRP, TOK), f32),
            vm((GRP, 8, MSG), f32), vm((GRP, 8, MSG), f32), vm((GRP, CHUNK, 128), bf16),
            vm((NBLK, SPAN, 2 * HEAD_DIM), bf16), vm((NBLK + 1, SPAN, 2 * HEAD_DIM), f32),
            vm((SPAN, 2 * HEAD_DIM), bf16), vm((SPAN, 2 * HEAD_DIM), bf16),
            vm((n, GRP, CHUNK, HEAD_DIM), bf16), vm((n, GRP, CHUNK, HEAD_DIM), bf16),
            vm((GRP, TOK, HEAD_DIM), bf16), vm((NBLK + 1, 1, SPAN), f32),
            vm((NBLK, SPAN, 2 * SPAN), f32), vm((NBLK, SPAN, 2 * SPAN), f32),
            dma((GRP,)), dma((GRP,)), dma((n,)), dma((n,)), dma((GRP,)), dma((GRP,)), dma((2,)),
            dma((n, 4)), dma((n, 4)), dma((1,)), dma((1,)),
            dma((GRP,)), dma((GRP,)), dma((ROUNDS,)), dma((ROUNDS,)), dma((GRP,)), dma((GRP,)),
            dma((1,)), dma((1,)), dma((n, 4)), dma((n, 4)), dma((GRP, ROUNDS)), dma((14,)),
        ],
        compiler_params=pltpu.CompilerParams(
            collective_id=0, has_side_effects=True, vmem_limit_bytes=60 * 1024 * 1024
        ),
        name="whole",
    )(q, k, v, g, inv, ordr, bucket, swap)


def finish_kernel(tiles, att, gq, gk, gv):
    for h in range(HEADS):
        att[:, h * HEAD_DIM:(h + 1) * HEAD_DIM] = tiles[h]
    for t, ref in enumerate((gq, gk, gv)):
        for n in range(2):
            ref[:, n * HEAD_DIM:(n + 1) * HEAD_DIM] = tiles[GRP + 2 * t + n]


def finish(tiles):
    part = jax.ShapeDtypeStruct((TOK, 2 * HEAD_DIM), bf16)
    return pl.pallas_call(
        finish_kernel,
        out_shape=(jax.ShapeDtypeStruct((TOK, HEADS * HEAD_DIM), bf16), part, part, part),
        name="finish",
    )(tiles)


def swap_matrix():
    at = np.arange(MSG)
    mirror = (at // SLOT % GRP) * CHUNK + (at // CHUNK) * SLOT + at % SLOT
    return (mirror[:, None] == at[None, :]).astype(jnp.bfloat16)


def on_device(queries, keys, values, cotangent, order, inverse, bucket):
    return finish(whole(queries, keys, values, cotangent, inverse, order,
                        bucket.reshape(GRP * NBLK, 1, SPAN), jnp.asarray(swap_matrix())))


def solution(mesh):
    return jax.shard_map(
        on_device,
        mesh=mesh,
        in_specs=(
            P("seq", None), P("seq", None), P("seq", None), P("seq", None),
            P("round", "seq"), P("round", "seq"), P("round", None),
        ),
        out_specs=(P("seq", None), P("seq", "round"), P("seq", "round"), P("seq", "round")),
        check_vma=False,
    )
```

```python
import jax
import jax.numpy as jnp
import numpy as np
from jax import lax
from jax.experimental import pallas as pl
from jax.experimental.pallas import tpu as pltpu
from jax.sharding import PartitionSpec as P

HEADS = 8
HEAD_DIM = 128
SPAN = 128
TOK = 256
SLOT = 6
GRP = 8
CHUNK = GRP * SLOT
MSG = GRP * CHUNK
ROUNDS = 4
ROWS = GRP * TOK
NBLK = ROWS // SPAN
NEG = -1e30
SCALE = HEAD_DIM ** (-0.5)
f32 = jnp.float32
bf16 = jnp.bfloat16
i32 = jnp.int32
ANY = pl.ANY


def here():
    x = lax.axis_index("round")
    s = lax.axis_index("seq")
    return x, lax.div(s, GRP), lax.rem(s, GRP)


def device(x, z, k):
    return {"seq": z * GRP + k, "round": x}


def remote(src, dst, send, recv, target):
    return pltpu.make_async_remote_copy(
        src_ref=src, dst_ref=dst, send_sem=send, recv_sem=recv,
        device_id=target, device_id_type=pl.DeviceIdType.MESH,
    )


def signal(sem, target):
    pl.semaphore_signal(sem, inc=1, device_id=target, device_id_type=pl.DeviceIdType.MESH)


def loop(lo, hi, body):
    def go(i, c):
        body(i)
        return c

    lax.fori_loop(lo, hi, go, 0)


def pairs(count, body):
    def go(i):
        body(2 * i)
        body(2 * i + 1)

    loop(0, count // 2, go)


def row_onehot(idx, count):
    places = lax.broadcasted_iota(i32, (count, TOK), 0)
    return jnp.where(places == idx, 1.0, 0.0).astype(bf16)


def col_of(idx):
    wide = jnp.broadcast_to(idx.astype(f32), (128, TOK))
    return jnp.concatenate([wide[:, :128].T, wide[:, 128:].T], axis=0).astype(i32)


def dot(a, b):
    return jnp.dot(a, b, preferred_element_type=f32)


def dot_nt(a, b):
    return lax.dot_general(a, b, (((1,), (1,)), ((), ())), preferred_element_type=f32)


def dot_tn(a, b):
    return lax.dot_general(a, b, (((0,), (0,)), ((), ())), preferred_element_type=f32)


def three(a):
    hi = a.astype(bf16)
    left = a - hi.astype(f32)
    mid = left.astype(bf16)
    low = (left - mid.astype(f32)).astype(bf16)
    return hi.astype(f32), mid.astype(f32), low.astype(f32)


def window(rows, tail, b):
    own = rows[b]
    if isinstance(b, int) and b == 0:
        before = tail[...]
    else:
        before = rows[b - 1][:, HEAD_DIM:3 * HEAD_DIM]
    keys = jnp.concatenate([before[:, :HEAD_DIM], own[:, HEAD_DIM:2 * HEAD_DIM]], axis=0)
    vals = jnp.concatenate([before[:, HEAD_DIM:], own[:, 2 * HEAD_DIM:3 * HEAD_DIM]], axis=0)
    return own[:, :HEAD_DIM], keys, vals, own[:, 3 * HEAD_DIM:]


def cols(ref, h):
    return ref.at[:, pl.ds(pl.multiple_of(h * HEAD_DIM, HEAD_DIM), HEAD_DIM)]


def both(copy):
    copy.wait_send()
    copy.wait_recv()


def ranks(col, row, before):
    return jnp.sum(jnp.where(jnp.logical_and(col == row, before), 1.0, 0.0), axis=0, keepdims=True)


def wide_col(row):
    col = col_of(row)
    return jnp.concatenate([col, col], axis=1)


def whole_kernel(
    q, k_, v, g_, inv, ordr, bucket, swap, final,
    sidx, ridx, sall, rall, zin, packed, recv, table, ohr, ohrt, ohst, mid, rows, tail,
    stat, smid, sent, got, across, reply, back, bmid, outq, outkv, spill_out, spill_in,
    packed2, recv2, settled, near, score, pgrad,
    zs, zr, ss, sr, rs, rr, ls, ps, pr, ts, tr, s1, r1, s2, r2, s3, r3, ws, wr, bs, br, hs, hr,
):
    x, z, k = here()
    line = x * GRP + z
    me = x * GRP + k
    total = 4 * GRP
    barrier = pltpu.get_barrier_semaphore()

    def on_line(i):
        o = lax.rem(line + i, total)
        return o, device(lax.div(o, GRP), lax.rem(o, GRP), k)

    def on_plane(i):
        o = lax.rem(me + i * 11, total)
        return o, device(lax.div(o, GRP), z, lax.rem(o, GRP))

    def greet(i):
        signal(barrier, on_line(i)[1])
        signal(barrier, on_plane(i)[1])

    loop(1, total, greet)
    mine = (z == k).astype(i32)

    def greet_pos(i):
        @pl.when(jnp.logical_or(z != k, i != z))
        def _():
            signal(barrier, device(x, i, z))

        @pl.when(jnp.logical_or(z != k, i != k))
        def _():
            signal(barrier, device(x, k, i))

    loop(0, GRP, greet_pos)

    for t, ref in enumerate((q, k_, v, g_)):
        @pl.when(x == t)
        def _(ref=ref):
            pltpu.make_async_copy(cols(ref, z), zin.at[z], ls.at[0]).start()

    up = lax.broadcasted_iota(i32, (TOK, TOK), 0)
    across_ = lax.broadcasted_iota(i32, (TOK, TOK), 1)
    target = lax.shift_right_logical(inv[...], 8)
    rank = ranks(wide_col(target), target, up < across_).astype(i32)
    sidx[...] = target * SLOT + rank
    tokens = ordr[...]
    source = lax.shift_right_logical(tokens, 8)
    rank = ranks(wide_col(source), source, wide_col(tokens) < tokens).astype(i32)
    part = jnp.bitwise_and(source, GRP - 1)
    ridx[...] = part * CHUNK + lax.shift_right_logical(source, 3) * SLOT + rank

    pl.semaphore_wait(barrier, 2 * (total - 1) + 2 * (GRP - mine))

    def send_idx(i):
        o, target_ = on_line(i)
        remote(sidx, sall.at[line], ss.at[o], sr.at[line], target_).start()

    loop(1, total, send_idx)
    sall[line] = sidx[...]

    for t, ref in enumerate((q, k_, v, g_)):
        @pl.when(x == t)
        def _(ref=ref):
            def go(i):
                step = lax.div(i + 1, 2)
                o = lax.rem(z + jnp.where(lax.rem(i, 2) == 1, step, GRP - step), GRP)
                remote(cols(ref, o), zin.at[z], zs.at[o], zr.at[z], device(x, o, k)).start()

            loop(1, GRP, go)

    def send_pos(i):
        @pl.when(jnp.logical_or(z != k, i != z))
        def _():
            remote(ridx, rall.at[k], rs.at[i], rr.at[k], device(x, i, z)).start()

    loop(0, GRP, send_pos)

    @pl.when(z == k)
    def _():
        rall[k] = ridx[...]

    def wait_idx(i):
        o, target_ = on_line(i)
        both(remote(sidx, sall.at[o], ss.at[o], sr.at[o], target_))

    loop(1, total, wait_idx)

    def pack_one(i):
        @pl.when(i == z)
        def _():
            pltpu.make_async_copy(cols(q, z), zin.at[z], ls.at[0]).wait()

        @pl.when(i != z)
        def _():
            both(remote(cols(q, i), zin.at[i], zs.at[i], zr.at[i], device(x, i, k)))

        def per_round(r):
            onehot = row_onehot(sall[r * GRP + i], MSG)
            value = dot(onehot, zin[i]).astype(bf16).reshape(GRP, CHUNK, HEAD_DIM)
            packed[pl.ds(r * GRP, GRP), i] = value

        loop(0, ROUNDS, per_round)

    def pack_pair(j):
        p = lax.rem(lax.div(z, 2) + j + lax.div(j, 2) - 2 * lax.div(j, 3), 4)
        pack_one(2 * p)
        pack_one(2 * p + 1)

        def go(i):
            o, target_ = on_plane(i)
            remote(packed.at[o, pl.ds(2 * p, 2)], recv.at[me, pl.ds(2 * p, 2)],
                   ps.at[o, p], pr.at[me, p], target_).start()

        loop(1, total, go)

    loop(0, 4, pack_pair)
    recv[me] = packed[me]

    def wait_pos(i):
        @pl.when(jnp.logical_or(z != k, i != z))
        def _():
            remote(ridx, rall.at[k], rs.at[i], rr.at[i], device(x, i, z)).wait_send()

        @pl.when(jnp.logical_or(z != k, i != k))
        def _():
            remote(ridx, rall.at[i], rs.at[i], rr.at[i], device(x, k, i)).wait_recv()

    loop(0, GRP, wait_pos)

    lanes = lax.broadcasted_iota(i32, (TOK, 128), 1)

    def fill_near(b):
        near[b] = bucket[lax.rem(k * NBLK + b + GRP * NBLK - 1, GRP * NBLK)].astype(f32)

    loop(0, NBLK + 1, fill_near)

    def fill_pos(d):
        col = col_of(rall[d])
        for m in range(3):
            ohr[d, :, m * 128:(m + 1) * 128] = jnp.where(col == lanes + m * 128, 1.0, 0.0).astype(bf16)
        ohrt[d] = row_onehot(rall[d], MSG)

    loop(0, GRP, fill_pos)

    def fill_tok(n):
        col = col_of(sall[n])
        for m in range(3):
            ohst[n, :, m * 128:(m + 1) * 128] = jnp.where(col == lanes + m * 128, 1.0, 0.0).astype(bf16)

    loop(0, total, fill_tok)

    def fill_table(i):
        table[:, i] = row_onehot(sall[x * GRP + i], MSG).reshape(GRP, CHUNK, TOK)

    loop(0, GRP, fill_table)

    def first(i):
        g = lax.rem(k + i, GRP)

        def arrived(n):
            t = lax.div(n, 4)
            p = lax.rem(n, 4)
            o = t * GRP + g

            @pl.when(o != me)
            def _():
                both(remote(packed.at[o, pl.ds(2 * p, 2)], recv.at[o, pl.ds(2 * p, 2)],
                            ps.at[o, p], pr.at[o, p], device(t, z, g)))

        loop(0, 16, arrived)
        parts = [recv[t * GRP + g].reshape(MSG, HEAD_DIM) for t in range(4)]
        moved = dot(swap[...], jnp.concatenate(parts, axis=1)).astype(bf16)
        mid[:, g] = moved.reshape(GRP, CHUNK, 4 * HEAD_DIM)

    loop(0, GRP, first)

    def second(d):
        value = dot(ohr[d], mid[d].reshape(MSG, 4 * HEAD_DIM)).astype(bf16)
        rows[pl.ds(2 * d, 2)] = value.reshape(2, SPAN, 4 * HEAD_DIM)

    second(GRP - 1)
    after = device(x, z, lax.rem(k + 1, GRP))
    before = device(x, z, lax.rem(k + GRP - 1, GRP))
    tail_copy = remote(rows.at[NBLK - 1, :, pl.ds(HEAD_DIM, 2 * HEAD_DIM)], tail, ts.at[0], tr.at[0],
                       after)
    tail_copy.start()
    loop(0, GRP - 1, second)

    def allowed_of(b):
        own = near[b + 1]
        col = jnp.broadcast_to(own, (SPAN, SPAN)).T
        return jnp.concatenate([col == near[b], col == own], axis=1)

    lane8 = jnp.bitwise_and(lax.broadcasted_iota(i32, (SPAN, 128), 1), 7)

    def forward(b):
        query, keys, vals, grad = window(rows, tail, b)
        allowed = allowed_of(b)
        scores = jnp.where(allowed, dot_nt(query, keys) * SCALE, NEG)
        score[b] = scores
        peak = jnp.max(scores, axis=-1, keepdims=True)
        expon = jnp.where(allowed, jnp.exp(scores - peak), 0.0)
        norm = jnp.sum(expon, axis=-1, keepdims=True)
        output = dot((expon / norm).astype(bf16), vals)
        lse = peak + jnp.log(norm)
        inner = jnp.sum(output * grad.astype(f32), axis=-1, keepdims=True)
        value = jnp.zeros((SPAN, 128), f32)
        for n, piece in enumerate(three(lse) + three(inner)):
            value = jnp.where(lane8 == n, piece, value)
        stat[b] = value.astype(bf16)

    def forward_three(j):
        for n in range(3):
            forward(1 + 3 * j + n)

    loop(0, 5, forward_three)
    both(tail_copy)
    forward(0)
    group = lax.shift_right_logical(lax.broadcasted_iota(i32, (CHUNK, 128), 1), 3)

    def stat_pack(d):
        moved = dot(ohrt[d], stat[pl.ds(2 * d, 2)].reshape(TOK, 128))
        value = jnp.zeros((CHUNK, 128), f32)
        for g in range(GRP):
            value = jnp.where(group == g, moved[g * CHUNK:(g + 1) * CHUNK], value)
        smid[d] = value.astype(bf16)

    pairs(GRP, stat_pack)
    sent[...] = dot(swap[...], smid[...].reshape(MSG, 128)).T[:8 * GRP].reshape(GRP, 8, MSG)

    def on_k(i):
        o = lax.rem(k + i, GRP)
        return o, device(x, z, o)

    def on_x(i):
        o = lax.rem(x + i, ROUNDS)
        return o, device(o, z, k)

    def go1(i):
        o, target_ = on_k(i)
        remote(sent.at[o], got.at[k], s1.at[o], r1.at[k], target_).start()

    loop(1, GRP, go1)
    got[k] = sent[k]

    def prob_grad_of(b):
        _, _, vals, grad = window(rows, tail, b)
        pgrad[b] = dot_nt(grad, vals)

    def prob_grad_three(j):
        for n in range(3):
            prob_grad_of(1 + 3 * j + n)

    prob_grad_of(0)
    loop(0, 5, prob_grad_three)

    def end1(i):
        o, target_ = on_k(i)
        both(remote(sent.at[o], got.at[o], s1.at[o], r1.at[o], target_))

    loop(1, GRP, end1)
    place = lax.broadcasted_iota(i32, (8, MSG), 1)
    start = lax.broadcasted_iota(i32, (8, MSG), 0) * CHUNK
    keep = jnp.logical_and(place >= start, place < start + CHUNK)

    def collect(o, acc):
        piece = got[o]
        wide = [jnp.where(keep, jnp.broadcast_to(piece[n:n + 1], (8, MSG)), 0.0) for n in range(6)]
        return acc + dot(jnp.concatenate(wide, axis=0).astype(bf16), table[o].reshape(MSG, TOK))

    tok = lax.fori_loop(0, GRP // 2, lambda i, acc: collect(2 * i + 1, collect(2 * i, acc)),
                        jnp.zeros((48, TOK), f32))
    across[x, 0] = tok[0:8] + tok[8:16] + tok[16:24]
    across[x, 1] = tok[24:32] + tok[32:40] + tok[40:48]

    def go2(i):
        o, target_ = on_x(i)
        remote(across.at[x], across.at[x], s2.at[o], r2.at[x], target_).start()

    loop(1, ROUNDS, go2)

    def end2(i):
        o, target_ = on_x(i)
        both(remote(across.at[x], across.at[o], s2.at[o], r2.at[o], target_))

    loop(1, ROUNDS, end2)
    lses = [across[r, 0] for r in range(ROUNDS)]
    top = jnp.maximum(jnp.maximum(lses[0], lses[1]), jnp.maximum(lses[2], lses[3]))
    exps = [jnp.exp(a - top) for a in lses]
    norm = (exps[0] + exps[1]) + (exps[2] + exps[3])
    joint = top + jnp.log(norm)
    delta = sum(exps[r] * across[r, 1] for r in range(ROUNDS)) / norm
    pieces = jnp.concatenate(three(joint) + three(delta), axis=0).astype(bf16)

    def answer(o):
        wide = dot_nt(pieces, table[o].reshape(MSG, TOK))
        parts = [jnp.sum(jnp.where(keep, wide[n * 8:(n + 1) * 8], 0.0), axis=0, keepdims=True)
                 for n in range(6)]
        parts += [jnp.zeros((2, MSG), f32)]
        reply[o] = jnp.concatenate(parts, axis=0)

    pairs(GRP, answer)

    def go3(i):
        o, target_ = on_k(i)
        remote(reply.at[o], back.at[k], s3.at[o], r3.at[k], target_).start()

    loop(1, GRP, go3)
    back[k] = reply[k]

    def end3(i):
        o, target_ = on_k(i)
        both(remote(reply.at[o], back.at[o], s3.at[o], r3.at[o], target_))

    loop(1, GRP, end3)
    flat = jnp.concatenate(
        [back[...].reshape(8 * GRP, MSG), jnp.zeros((128 - 8 * GRP, MSG), f32)], axis=0
    )
    bmid[...] = dot(swap[...], flat.T.astype(bf16)).astype(bf16).reshape(GRP, CHUNK, 128)
    lane_tok = jnp.bitwise_and(lanes, 7)

    def joint_of(d):
        part_ = bmid[d].astype(f32)
        wide = jnp.concatenate(
            [jnp.where(group == g, part_, 0.0) for g in range(GRP)], axis=0
        ).astype(bf16)
        found = dot(ohr[d], wide)
        lse = jnp.sum(jnp.where(lane_tok < 3, found, 0.0), axis=-1, keepdims=True)
        dlt = jnp.sum(jnp.where(jnp.logical_and(lane_tok >= 3, lane_tok < 6), found, 0.0),
                      axis=-1, keepdims=True)
        return lse, dlt

    outkv[0] = jnp.zeros((SPAN, 2 * HEAD_DIM), f32)

    def backward(b, lse, dlt):
        query, keys, vals, grad = window(rows, tail, b)
        prob = jnp.exp(score[b] - lse)
        low = prob.astype(bf16)
        value_grad = dot_tn(low, grad)
        score_grad = (prob * (pgrad[b] - dlt)).astype(bf16)
        query_grad = dot(score_grad, keys) * SCALE
        key_grad = dot_tn(score_grad, query) * SCALE
        outq[b] = jnp.concatenate([dot(low, vals), query_grad], axis=1).astype(bf16)
        pair = jnp.concatenate([key_grad, value_grad], axis=1)
        outkv[b] = outkv[b] + pair[:SPAN]
        outkv[b + 1] = pair[SPAN:]

    def backward_pair(d):
        lse, dlt = joint_of(d)
        backward(2 * d, lse[:SPAN], dlt[:SPAN])
        backward(2 * d + 1, lse[SPAN:], dlt[SPAN:])

    backward_pair(0)
    spill_out[...] = outkv[0].astype(bf16)
    spill_copy = remote(spill_out, spill_in, ws.at[0], wr.at[0], before)
    spill_copy.start()
    loop(1, GRP, backward_pair)

    def repack(d):
        upper = jnp.concatenate([outq[2 * d], outkv[2 * d + 1].astype(bf16)], axis=1)
        lower = jnp.concatenate([outq[2 * d + 1], outkv[2 * d + 2].astype(bf16)], axis=1)
        moved = dot(ohrt[d], jnp.concatenate([upper, lower], axis=0)).astype(bf16)
        mid[:, d] = moved.reshape(GRP, CHUNK, 4 * HEAD_DIM)

    loop(0, GRP - 1, repack)
    both(spill_copy)
    outkv[NBLK] = outkv[NBLK] + spill_in[...].astype(f32)
    repack(GRP - 1)

    def reorder(g):
        moved = dot(swap[...], mid[g].reshape(MSG, 4 * HEAD_DIM)).astype(bf16)
        for i in range(GRP):
            for t in range(4):
                owner = lax.rem(t - i - z + 16, 4)
                packed2[owner * GRP + g, i] = moved[i * CHUNK:(i + 1) * CHUNK,
                                                    t * HEAD_DIM:(t + 1) * HEAD_DIM]

    loop(0, GRP, reorder)

    def back_pair(j):
        p = lax.rem(lax.div(z, 2) + j, 4)

        def go(i):
            o, target_ = on_plane(i)
            remote(packed2.at[o, pl.ds(2 * p, 2)], recv2.at[me, pl.ds(2 * p, 2)],
                   bs.at[o, p], br.at[me, p], target_).start()

        loop(1, total, go)

    loop(0, 4, back_pair)
    recv2[me] = packed2[me]
    owner = lax.div(z, 2)
    side = lax.rem(z, 2)

    def home(i, begin):
        kind = lax.rem(x + i + z, 4)

        @pl.when(kind == 0)
        def _():
            for o in range(ROUNDS):
                own = jnp.logical_and(x == o, z == i)

                @pl.when(jnp.logical_not(own))
                def _(o=o):
                    cp = remote(settled.at[i], final.at[z], hs.at[i, o], hr.at[z], device(o, i, k))
                    cp.start() if begin else cp.wait_send()

                @pl.when(own)
                def _():
                    cp = pltpu.make_async_copy(settled.at[i], final.at[z], ls.at[1])
                    cp.start() if begin else cp.wait()

        tile = GRP + 2 * (kind - 1) + side
        own = jnp.logical_and(x == owner, z == i)

        @pl.when(jnp.logical_and(kind != 0, jnp.logical_not(own)))
        def _():
            cp = remote(settled.at[i], final.at[tile], hs.at[i, 0], hr.at[tile], device(owner, i, k))
            cp.start() if begin else cp.wait_send()

        @pl.when(jnp.logical_and(kind != 0, own))
        def _():
            cp = pltpu.make_async_copy(settled.at[i], final.at[tile], ls.at[1])
            cp.start() if begin else cp.wait()

    def settle(i):
        acc = jnp.zeros((TOK, HEAD_DIM), f32)
        for r in range(ROUNDS):
            acc = acc + dot(ohst[r * GRP + i], recv2[r * GRP:(r + 1) * GRP, i].reshape(MSG, HEAD_DIM))
        settled[i] = acc.astype(bf16)
        home(i, True)

    def settle_pair(j):
        p = lax.rem(lax.div(z, 2) + j, 4)

        def end(i):
            o, target_ = on_plane(i)
            both(remote(packed2.at[o, pl.ds(2 * p, 2)], recv2.at[o, pl.ds(2 * p, 2)],
                        bs.at[o, p], br.at[o, p], target_))

        loop(1, total, end)
        loop(2 * p, 2 * p + 2, settle)

    loop(0, 4, settle_pair)
    loop(0, GRP, lambda i: home(i, False))

    def arrive(tile, kind, h):
        sender = lax.rem(32 + kind - z - h, 4)

        @pl.when(jnp.logical_not(jnp.logical_and(h == z, sender == x)))
        def _():
            remote(settled.at[0], final.at[tile], hs.at[0, 0], hr.at[tile],
                   device(sender, h, k)).wait_recv()

    loop(0, GRP, lambda h: arrive(h, 0, h))
    loop(0, 6, lambda n: arrive(GRP + n, 1 + lax.div(n, 2), 2 * x + lax.rem(n, 2)))


def whole(q, k, v, g, inv, ordr, bucket, swap):
    n = 4 * GRP
    dma = pltpu.SemaphoreType.DMA
    vm = pltpu.VMEM
    spec = pl.BlockSpec(memory_space=pltpu.VMEM)
    wide = 4 * HEAD_DIM
    return pl.pallas_call(
        whole_kernel,
        out_shape=jax.ShapeDtypeStruct((14, TOK, HEAD_DIM), bf16),
        in_specs=[pl.BlockSpec(memory_space=ANY)] * 4 + [spec] * 4,
        out_specs=pl.BlockSpec(memory_space=ANY),
        scratch_shapes=[
            vm((1, TOK), i32), vm((1, TOK), i32), vm((n, 1, TOK), i32), vm((GRP, 1, TOK), i32),
            vm((GRP, TOK, HEAD_DIM), bf16),
            vm((n, GRP, CHUNK, HEAD_DIM), bf16), vm((n, GRP, CHUNK, HEAD_DIM), bf16),
            vm((GRP, GRP, CHUNK, TOK), bf16), vm((GRP, TOK, MSG), bf16), vm((GRP, MSG, TOK), bf16),
            vm((n, TOK, MSG), bf16), vm((GRP, GRP, CHUNK, wide), bf16),
            vm((NBLK, SPAN, wide), bf16), vm((SPAN, 2 * HEAD_DIM), bf16),
            vm((NBLK, SPAN, 128), bf16), vm((GRP, CHUNK, 128), bf16),
            vm((GRP, 8, MSG), f32), vm((GRP, 8, MSG), f32), vm((ROUNDS, 2, GRP, TOK), f32),
            vm((GRP, 8, MSG), f32), vm((GRP, 8, MSG), f32), vm((GRP, CHUNK, 128), bf16),
            vm((NBLK, SPAN, 2 * HEAD_DIM), bf16), vm((NBLK + 1, SPAN, 2 * HEAD_DIM), f32),
            vm((SPAN, 2 * HEAD_DIM), bf16), vm((SPAN, 2 * HEAD_DIM), bf16),
            vm((n, GRP, CHUNK, HEAD_DIM), bf16), vm((n, GRP, CHUNK, HEAD_DIM), bf16),
            vm((GRP, TOK, HEAD_DIM), bf16), vm((NBLK + 1, 1, SPAN), f32),
            vm((NBLK, SPAN, 2 * SPAN), f32), vm((NBLK, SPAN, 2 * SPAN), f32),
            dma((GRP,)), dma((GRP,)), dma((n,)), dma((n,)), dma((GRP,)), dma((GRP,)), dma((2,)),
            dma((n, 4)), dma((n, 4)), dma((1,)), dma((1,)),
            dma((GRP,)), dma((GRP,)), dma((ROUNDS,)), dma((ROUNDS,)), dma((GRP,)), dma((GRP,)),
            dma((1,)), dma((1,)), dma((n, 4)), dma((n, 4)), dma((GRP, ROUNDS)), dma((14,)),
        ],
        compiler_params=pltpu.CompilerParams(
            collective_id=0, has_side_effects=True, vmem_limit_bytes=60 * 1024 * 1024
        ),
        name="whole",
    )(q, k, v, g, inv, ordr, bucket, swap)


def finish_kernel(tiles, att, gq, gk, gv):
    for h in range(HEADS):
        att[:, h * HEAD_DIM:(h + 1) * HEAD_DIM] = tiles[h]
    for t, ref in enumerate((gq, gk, gv)):
        for n in range(2):
            ref[:, n * HEAD_DIM:(n + 1) * HEAD_DIM] = tiles[GRP + 2 * t + n]


def finish(tiles):
    part = jax.ShapeDtypeStruct((TOK, 2 * HEAD_DIM), bf16)
    return pl.pallas_call(
        finish_kernel,
        out_shape=(jax.ShapeDtypeStruct((TOK, HEADS * HEAD_DIM), bf16), part, part, part),
        name="finish",
    )(tiles)


def swap_matrix():
    at = np.arange(MSG)
    mirror = (at // SLOT % GRP) * CHUNK + (at // CHUNK) * SLOT + at % SLOT
    return (mirror[:, None] == at[None, :]).astype(jnp.bfloat16)


def on_device(queries, keys, values, cotangent, order, inverse, bucket):
    return finish(whole(queries, keys, values, cotangent, inverse, order,
                        bucket.reshape(GRP * NBLK, 1, SPAN), jnp.asarray(swap_matrix())))


def solution(mesh):
    return jax.shard_map(
        on_device,
        mesh=mesh,
        in_specs=(
            P("seq", None), P("seq", None), P("seq", None), P("seq", None),
            P("round", "seq"), P("round", "seq"), P("round", None),
        ),
        out_specs=(P("seq", None), P("seq", "round"), P("seq", "round"), P("seq", "round")),
        check_vma=False,
    )
```
